128 devices in a mesh: lon: 64 (over y_lo, x, z, core), lat: 2 (over y_hi).
Axes of the slice: x: 4, y: 4 (y_hi: 2, y_lo: 2; y = y_hi * 2 + y_lo), z: 4, core: 2. Of those that a mesh axis runs over, the one named last changes fastest.
Arguments:
- tracers: float32 [3, 10, 128, 8192], P(None, None, 'lat', 'lon'), may hold values from -6 to 6
- offsets: int32 [10, 128, 8192], P(None, 'lat', 'lon'), may hold values from -16 to 15, as said below
- weights: float32 [10, 128, 8192], P(None, 'lat', 'lon'), may hold values from 0 to 1
- diffusion: float32 [9, 128, 8192], P(None, 'lat', 'lon'), may hold values from 0.05 to 5
- send_index: int32 [128, 128, 128], P(('lon', 'lat')), may hold values from 0 to 8191, as said below
- send_count: int32 [128, 128], P(('lon', 'lat')), may hold values from 1 to 128, as said below
Outputs:
- owned_tracers: float32 [3, 10, 1048576], P(None, None, ('lon', 'lat'))
The draws below stay inside these ranges and needn't reach their ends.
Inputs may be any that keep to these rules, and one draw needn't show every extreme that they name: `offsets`: the departure interval of a cell starts this many cells east of it on the same row and level; both ends of the range occur. `send_count`: entry [d, e] counts the columns of device d that device e owns. Every row and every column sums to 8192. A device keeps exactly 127 of its own columns and sends exactly one to the device 128 // 2 further on; some list holds exactly 128 columns. `send_index`: entries [d, e, 0 : send_count[d, e]] are local column indices of device d that device e owns, in owner order; each column of d appears in exactly one list once; entries past the count are valid column indices that carry no meaning.
All inputs are finite; a program needn't handle non-finite values.
Results may differ from the reference program's by a relative error of at most 0.0003.
Values sent between devices are 32-bit elements; how exact they have to be, the bound alone decides.
A program may use at most 128 MiB of HBM per device.

```python
import math
import jax
import jax.numpy as jnp
import numpy as np
from jax import lax

NTR = 3
LEV = 10
HALO = 16
CLAT = 64
CLON = 128
NLAT = 128
NLON = 8192
COLS_DEV = 8192
CAP = 128
N_LON = 64
N_LAT = 2
DEVICES = 128


def draw_offsets(key, part):
    half_reach = HALO // 2
    row_base = jax.random.randint(jax.random.fold_in(key, 21), (LEV, NLAT, 1), -half_reach, half_reach)
    wobble = jax.random.randint(jax.random.fold_in(key, 22), (LEV, NLAT, NLON), -half_reach, half_reach + 1)
    result = (row_base + wobble).astype(jnp.int32)
    result = jnp.clip(result, -HALO, HALO - 1).astype(jnp.int32)
    result = result.at[0, 0, 0].set(-HALO)
    result = result.at[0, 0, NLON - 1].set(HALO - 1)
    return result


def route_counts(key):
    half_count = DEVICES // 2
    base_half = jax.random.randint(jax.random.fold_in(key, 11), (half_count,), 2, CAP - 1)
    base_half = base_half.at[0].set(CAP - 1)
    base_half = base_half.at[2].set(CAP - 2)
    by_offset = jnp.concatenate([base_half, CAP - base_half]).astype(jnp.int32)
    per_device = jnp.broadcast_to(by_offset[None, :], (DEVICES, DEVICES))
    triple_starts = np.concatenate([np.arange(1, half_count, 3), np.arange(half_count + 1, DEVICES, 3)])
    flips = jax.random.randint(jax.random.fold_in(key, 12), (triple_starts.shape[0], DEVICES), 0, 2).astype(jnp.int32)
    flips = flips.at[0, 0].set(1)
    flips = flips.at[0, 1].set(1)
    flips_next = jnp.roll(flips, -1, axis=1)
    delta = jnp.zeros((DEVICES, DEVICES), jnp.int32)
    delta = delta.at[:, triple_starts + 1].add((flips + flips_next).T)
    delta = delta.at[:, triple_starts].add(-flips.T)
    delta = delta.at[:, triple_starts + 2].add(-flips_next.T)
    per_device = per_device + delta
    rank_index = jnp.arange(DEVICES, dtype=jnp.int32)
    offset_table = (rank_index[None, :] - rank_index[:, None]) % DEVICES
    return jnp.take_along_axis(per_device, offset_table, axis=1).astype(jnp.int32)


def draw_send_count(key, part):
    return route_counts(key)


def draw_send_index(key, part):
    counts = route_counts(key)
    device_keys = jax.random.split(jax.random.fold_in(key, 13), DEVICES)
    shuffles = jax.vmap(lambda one_key: jax.random.permutation(one_key, COLS_DEV))(device_keys).astype(jnp.int32)
    starts = jnp.cumsum(counts, axis=1) - counts
    slots = starts[:, :, None] + jnp.arange(CAP, dtype=jnp.int32)[None, None, :]
    slots = jnp.minimum(slots, COLS_DEV - 1)
    return jax.vmap(lambda shuffle, slot_rows: shuffle[slot_rows])(shuffles, slots).astype(jnp.int32)


def steps_of(key, shape, cuts, least, largest):
    level, own = 1.0, jax.random.fold_in(key, 6)
    for axis_at, parts in cuts:
        heights = jnp.exp(jax.random.uniform(jax.random.fold_in(own, axis_at), (parts,), jnp.float32, least / len(cuts), largest / len(cuts)))
        level = level * jnp.repeat(heights, shape[axis_at] // parts).reshape([-1 if axis == axis_at else 1 for axis in range(len(shape))])
    return level


def bell_draw(key, dims, scale, reach, cuts=(), kind=jnp.bfloat16):
    drawn = jax.random.normal(key, dims, jnp.float32) * scale
    if len(cuts) > 0:
        drawn = steps_of(key, dims, cuts, -0.22, 0.18) * drawn
    return jnp.clip(drawn, min=-reach, max=reach).astype(kind)


def setup_inputs(seed: int = 0) -> dict:
    streams_of = jax.random.split(jax.random.key(seed), 7)
    return {
        "tracers": bell_draw(streams_of[0], (NTR, LEV, NLAT, NLON), 1.0, 6.0, ((2, 2), (3, 64)), jnp.float32),
        "offsets": draw_offsets(jax.random.fold_in(streams_of[6], 71), 0),
        "weights": jnp.clip(1.0 * jax.random.uniform(streams_of[2], (LEV, NLAT, NLON), jnp.float32) ** steps_of(streams_of[2], (LEV, NLAT, NLON), ((1, 2), (2, 64)), -0.2, 0.2), 0.0, 1.0),
        "diffusion": jnp.clip(jnp.exp(math.log(5.0) - 4.6051702 * jax.random.uniform(streams_of[3], (LEV - 1, NLAT, NLON), jnp.float32) ** steps_of(streams_of[3], (LEV - 1, NLAT, NLON), ((1, 2), (2, 64)), -0.2, 0.2)), 0.05, 5.0),
        "send_index": draw_send_index(jax.random.fold_in(streams_of[6], 71), 0),
        "send_count": draw_send_count(jax.random.fold_in(streams_of[6], 71), 0),
    }


def solve_columns(values, coef_rows):
    levels = values.shape[1]
    diag = []
    for level in range(levels):
        term = jnp.ones_like(coef_rows[0])
        if level > 0:
            term = term + coef_rows[level - 1]
        if level < levels - 1:
            term = term + coef_rows[level]
        diag.append(term)
    upper = []
    reduced = []
    denom = diag[0]
    upper.append(-coef_rows[0] / denom)
    reduced.append(values[:, 0] / denom)
    for level in range(1, levels):
        denom = diag[level] + coef_rows[level - 1] * upper[level - 1]
        reduced.append((values[:, level] + coef_rows[level - 1] * reduced[level - 1]) / denom)
        if level < levels - 1:
            upper.append(-coef_rows[level] / denom)
    output = [None] * levels
    output[levels - 1] = reduced[levels - 1]
    for level in range(levels - 2, -1, -1):
        output[level] = reduced[level] - upper[level] * output[level + 1]
    return jnp.stack(output, axis=1)


def to_devices(field):
    lead = field.shape[0]
    shaped = field.reshape(lead, N_LAT, CLAT, N_LON, CLON)
    shaped = jnp.transpose(shaped, (0, 3, 1, 2, 4))
    return shaped.reshape(lead, N_LON * N_LAT, CLAT * CLON)


def reference(tracers, offsets, weights, diffusion, send_index, send_count):
    nlon_cells = tracers.shape[3]
    cell_index = jnp.arange(nlon_cells, dtype=jnp.int32)
    left_index = ((offsets + cell_index[None, None, :]) % nlon_cells).astype(jnp.int32)
    right_index = ((left_index + 1) % nlon_cells).astype(jnp.int32)
    full_shape = tracers.shape
    left_value = jnp.take_along_axis(tracers, jnp.broadcast_to(left_index[None], full_shape), axis=3)
    right_value = jnp.take_along_axis(tracers, jnp.broadcast_to(right_index[None], full_shape), axis=3)
    advected = (1.0 - weights)[None] * left_value + weights[None] * right_value
    by_device = to_devices(advected.reshape(NTR * LEV, NLAT, NLON))
    coef_device = to_devices(diffusion)

    def owner_columns(destination):
        offset_rank = jnp.arange(DEVICES, dtype=jnp.int32)
        sources = ((destination - offset_rank) % DEVICES).astype(jnp.int32)
        counts = send_count[sources, destination]
        seg_ends = jnp.cumsum(counts)
        places = jnp.arange(COLS_DEV, dtype=jnp.int32)
        passed = seg_ends[:, None] <= places[None, :]
        segment = jnp.sum(passed.astype(jnp.int32), axis=0).astype(jnp.int32)
        seg_start = jnp.sum(jnp.where(passed, counts[:, None], 0), axis=0).astype(jnp.int32)
        source = ((destination - segment) % DEVICES).astype(jnp.int32)
        column = send_index[source, destination, (places - seg_start).astype(jnp.int32)]
        return source, column.astype(jnp.int32)

    sources, columns = lax.map(owner_columns, jnp.arange(DEVICES, dtype=jnp.int32))
    gathered = by_device[:, sources, columns].reshape(NTR, LEV, DEVICES * COLS_DEV)
    gathered_diffusion = coef_device[:, sources, columns].reshape(LEV - 1, DEVICES * COLS_DEV)
    return solve_columns(gathered, gathered_diffusion)
```

```python
import jax
import jax.numpy as jnp
from jax import lax
from jax.experimental import pallas as pl
from jax.experimental.pallas import tpu as pltpu
from jax.sharding import PartitionSpec as P

NTR = 3
LEV = 10
HALO = 16
FEAT = 32
LANES = 128
AXES = ("lon", "lat")


def shifted(block, axis, distance):
    devices = range(lax.axis_size(axis))
    route = [((i - distance) % len(devices), i) for i in devices]
    return lax.ppermute(block, axis, route)


def solve_levels(values, coefs):
    upper, reduced = [], [[] for _ in values]
    for level in range(LEV):
        denom = jnp.ones_like(coefs[0])
        if level > 0:
            denom = denom + coefs[level - 1]
        if level < LEV - 1:
            denom = denom + coefs[level]
        if level > 0:
            denom = denom - coefs[level - 1] * upper[level - 1]
        inverse = 1.0 / denom
        if level < LEV - 1:
            upper.append(coefs[level] * inverse)
        for t in range(len(values)):
            right = values[t][level]
            if level > 0:
                right = right + coefs[level - 1] * reduced[t][level - 1]
            reduced[t].append(right * inverse)
    output = [[None] * LEV for _ in values]
    for t in range(len(values)):
        output[t][LEV - 1] = reduced[t][LEV - 1]
        for level in range(LEV - 2, -1, -1):
            output[t][level] = reduced[t][level] + upper[level] * output[t][level + 1]
    return output


def pack_kernel(tracers, halo, offsets, weights, diffusion, index, count, packed, rows, table, stage):
    lat_rows = tracers.shape[2]
    peers = packed.shape[0]
    lane = lax.broadcasted_iota(jnp.int32, (8, LANES), 1)

    def advect_group(group, carry):
        at = pl.ds(pl.multiple_of(group * 8, 8), 8)
        values = [[] for _ in range(NTR)]
        for level in range(LEV):
            cell = lane + offsets[level, at, :]
            weight = weights[level, at, :]
            west_in = (cell >= 0) & (cell < LANES)
            west_at = cell & (LANES - 1)
            east_in = (cell >= -1) & (cell < LANES - 1)
            east_at = (cell + 1) & (LANES - 1)
            for t in range(NTR):
                main = tracers[t, level, at, :]
                edge = halo[t, level, at, :]
                west = jnp.where(
                    west_in,
                    jnp.take_along_axis(main, west_at, axis=1),
                    jnp.take_along_axis(edge, west_at, axis=1),
                )
                east = jnp.where(
                    east_in,
                    jnp.take_along_axis(main, east_at, axis=1),
                    jnp.take_along_axis(edge, east_at, axis=1),
                )
                values[t].append((1.0 - weight) * west + weight * east)
        coefs = [diffusion[level, at, :] for level in range(LEV - 1)]
        solved = solve_levels(values, coefs)
        for t in range(NTR):
            for level in range(LEV):
                rows[pl.ds(group * 8 * FEAT + t * LEV + level, 8, stride=FEAT), :] = solved[t][level]
        for spare in range(NTR * LEV, FEAT):
            rows[pl.ds(group * 8 * FEAT + spare, 8, stride=FEAT), :] = jnp.zeros((8, LANES), jnp.float32)
        return carry

    lax.fori_loop(0, lat_rows // 8, advect_group, 0)

    def turn(row, carry):
        block = rows[pl.ds(pl.multiple_of(row * FEAT, FEAT), FEAT), :]
        wide = jnp.concatenate([block] * (LANES // FEAT), axis=0)
        table[pl.ds(pl.multiple_of(row * LANES, LANES), LANES), :] = wide.T
        return carry

    lax.fori_loop(0, lat_rows, turn, 0)

    four = LANES // FEAT
    lane_group = lax.broadcasted_iota(jnp.int32, (LANES, LANES), 1) // FEAT

    def pick(step, carry):
        for slot in range(LANES):
            for member in range(four):
                column = index[step * four + member, slot]
                stage[member, slot : slot + 1, :] = table[pl.ds(column, 1), :]
        wide = stage[0]
        for member in range(1, four):
            wide = jnp.where(lane_group == member, stage[member], wide)
        turned = wide.T
        for member in range(four):
            packed[step * four + member] = turned[member * FEAT : (member + 1) * FEAT, :]
            length = count[0, step * four + member].astype(jnp.float32)
            packed[step * four + member, NTR * LEV : NTR * LEV + 1, :] = jnp.full((1, LANES), length, jnp.float32)
        return carry

    lax.fori_loop(0, peers // four, pick, 0)


def place_kernel(arrived, counts, out, owned):
    peers = arrived.shape[0]
    columns = out.shape[2]
    me = lax.axis_index(AXES)
    lane = lax.broadcasted_iota(jnp.int32, (FEAT, LANES), 1)

    def place(step, start):
        source = lax.rem(me - step + peers, peers)
        block = start // LANES
        shift = lax.rem(start, LANES)
        rolled = pltpu.roll(arrived[source], shift, 1)
        first = pl.ds(pl.multiple_of(block * FEAT, FEAT), FEAT)
        second = pl.ds(pl.multiple_of(block * FEAT + FEAT, FEAT), FEAT)
        owned[first, :] = jnp.where(lane >= shift, rolled, owned[first, :])
        owned[second, :] = rolled
        return start + counts[source]

    lax.fori_loop(0, peers, place, jnp.int32(0))

    for block in range(columns // LANES):
        for t in range(NTR):
            begin = block * FEAT + t * LEV
            out[t, :, block * LANES : (block + 1) * LANES] = owned[begin : begin + LEV, :]


def body(tracers, offsets, weights, diffusion, send_index, send_count):
    lat_rows, lon_width = tracers.shape[2:]
    peers = lax.axis_size(AXES)
    columns = lat_rows * lon_width
    from_west = shifted(tracers[..., lon_width - HALO :], "lon", 1)
    from_east = shifted(tracers[..., :HALO], "lon", -1)
    middle = jnp.zeros((*tracers.shape[:3], lon_width - 2 * HALO), jnp.float32)
    halo = jnp.concatenate([from_east, middle, from_west], axis=3)
    vmem = pl.BlockSpec(memory_space=pltpu.VMEM)
    smem = pl.BlockSpec(memory_space=pltpu.SMEM)
    packed = pl.pallas_call(
        pack_kernel,
        out_shape=jax.ShapeDtypeStruct((peers, FEAT, LANES), jnp.float32),
        in_specs=[vmem] * 5 + [smem] * 2,
        out_specs=vmem,
        scratch_shapes=[
            pltpu.VMEM((lat_rows * FEAT, LANES), jnp.float32),
            pltpu.VMEM((columns, LANES), jnp.float32),
            pltpu.VMEM((LANES // FEAT, LANES, LANES), jnp.float32),
        ],
        compiler_params=pltpu.CompilerParams(vmem_limit_bytes=40 << 20),
        name="advect_solve_pack",
    )(tracers, halo, offsets, weights, diffusion, send_index[0], send_count)
    arrived = lax.all_to_all(packed, AXES, split_axis=0, concat_axis=0, tiled=True)
    counts = arrived[:, NTR * LEV, 0].astype(jnp.int32)
    return pl.pallas_call(
        place_kernel,
        out_shape=jax.ShapeDtypeStruct((NTR, LEV, columns), jnp.float32),
        in_specs=[vmem, smem],
        out_specs=vmem,
        scratch_shapes=[pltpu.VMEM(((columns // LANES + 2) * FEAT, LANES), jnp.float32)],
        compiler_params=pltpu.CompilerParams(vmem_limit_bytes=32 << 20),
        name="place_owned",
    )(arrived, counts)


def solution(mesh):
    return jax.shard_map(
        body,
        mesh=mesh,
        in_specs=(
            P(None, None, "lat", "lon"),
            P(None, "lat", "lon"),
            P(None, "lat", "lon"),
            P(None, "lat", "lon"),
            P(("lon", "lat"), None, None),
            P(("lon", "lat"), None),
        ),
        out_specs=P(None, None, ("lon", "lat")),
        check_vma=False,
    )
```

```python
import jax
import jax.numpy as jnp
from jax import lax
from jax.experimental import pallas as pl
from jax.experimental.pallas import tpu as pltpu
from jax.sharding import PartitionSpec as P

NTR = 3
LEV = 10
HALO = 16
FEAT = 32
SENT = NTR * LEV + 1
LANES = 128
FOUR = LANES // FEAT
EDGES = LANES // HALO
PEERS = 128
AXES = ("lon", "lat")
MESH = pl.DeviceIdType.MESH


def torus_target(lon, lat, shift, flip):
    x, y, z, core = (lon // 8) % 4, lat * 2 + lon // 32, (lon // 2) % 4, lon % 2
    x = (x + shift) % 4
    y = (y + shift // 4 + shift) % 4
    z = (z + shift // 16 + shift // 4 + shift) % 4
    core = (core + flip) % 2
    return (y % 2) * 32 + x * 8 + z * 2 + core, y // 2


def solve_levels(values, coefs):
    upper, reduced = [], [[] for _ in values]
    for level in range(LEV):
        denom = jnp.ones_like(coefs[0])
        if level > 0:
            denom = denom + coefs[level - 1]
        if level < LEV - 1:
            denom = denom + coefs[level]
        if level > 0:
            denom = denom - coefs[level - 1] * upper[level - 1]
        inverse = 1.0 / denom
        if level < LEV - 1:
            upper.append(coefs[level] * inverse)
        for t in range(len(values)):
            right = values[t][level]
            if level > 0:
                right = right + coefs[level - 1] * reduced[t][level - 1]
            reduced[t].append(right * inverse)
    output = [[None] * LEV for _ in values]
    for t in range(len(values)):
        output[t][LEV - 1] = reduced[t][LEV - 1]
        for level in range(LEV - 2, -1, -1):
            output[t][level] = reduced[t][level] + upper[level] * output[t][level + 1]
    return output


def exchange_kernel(
    tracers, offsets, weights, diffusion, index, count, arrived, lengths,
    edge_low, edge_high, from_east, from_west, rows, table, stage, outbox, place, address,
    edge_sems, address_sem, send_sem, recv_sem,
):
    lat_rows = tracers.shape[2]
    groups = lat_rows // 8
    packs = from_east.shape[1]
    lon, lat = lax.axis_index("lon"), lax.axis_index("lat")
    bands = lax.axis_size("lon")
    me = lon * 2 + lat
    lane = lax.broadcasted_iota(jnp.int32, (8, LANES), 1)
    lane_group = lax.broadcasted_iota(jnp.int32, (LANES, LANES), 1) // FEAT

    barrier = pltpu.get_barrier_semaphore()

    def greet(other, carry):
        to_lon, to_lat = torus_target(lon, lat, other // 2, other % 2)
        pl.semaphore_signal(barrier, inc=1, device_id=(to_lon, to_lat), device_id_type=MESH)
        return carry

    lax.fori_loop(1, PEERS, greet, 0)

    def pack_edges(group, carry):
        at = pl.ds(pl.multiple_of(group * 8, 8), 8)
        for pack in range(packs):
            low = high = None
            for part in range(EDGES):
                plane = pack * EDGES + part
                if plane >= NTR * LEV:
                    continue
                value = tracers[plane // LEV, plane % LEV, at, :]
                to_low = pltpu.roll(value, part * HALO, 1) if part else value
                to_high = pltpu.roll(value, (part + 1) * HALO, 1) if part + 1 < EDGES else value
                inside = lane // HALO == part
                low = to_low if part == 0 else jnp.where(inside, to_low, low)
                high = to_high if part == 0 else jnp.where(inside, to_high, high)
            edge_low[group, pack] = low
            edge_high[group, pack] = high
        return carry

    lax.fori_loop(0, groups, pack_edges, 0)

    column = index[...]
    owner = lax.broadcasted_iota(jnp.int32, column.shape, 0)
    member_of = ((owner // 16) % 4 - (lon // 8) % 4 + 4) % 4
    row = column // LANES
    turn_by = (member_of - row % 4 + 4) % 4
    place[...] = turn_by * (lat_rows * LANES // 4) + (row // 4) * LANES + column % LANES
    to_scalars = pltpu.make_async_copy(place, address, address_sem)
    to_scalars.start()

    pl.semaphore_wait(barrier, PEERS - 1)
    to_west = pltpu.make_async_remote_copy(
        src_ref=edge_low, dst_ref=from_east, send_sem=edge_sems.at[0], recv_sem=edge_sems.at[1],
        device_id=(lax.rem(lon + bands - 1, bands), lat), device_id_type=MESH,
    )
    to_east = pltpu.make_async_remote_copy(
        src_ref=edge_high, dst_ref=from_west, send_sem=edge_sems.at[2], recv_sem=edge_sems.at[3],
        device_id=(lax.rem(lon + 1, bands), lat), device_id_type=MESH,
    )
    to_west.start()
    to_east.start()
    to_west.wait()
    to_east.wait()

    def advect_group(group, carry):
        at = pl.ds(pl.multiple_of(group * 8, 8), 8)
        values = [[] for _ in range(NTR)]
        for level in range(LEV):
            cell = lane + offsets[level, at, :]
            weight = weights[level, at, :]
            west_in = (cell >= 0) & (cell < LANES)
            west_at = cell & (LANES - 1)
            east_in = (cell >= -1) & (cell < LANES - 1)
            east_at = (cell + 1) & (LANES - 1)
            for t in range(NTR):
                plane = t * LEV + level
                pack, part = plane // EDGES, plane % EDGES
                main = tracers[t, level, at, :]
                right = from_east[group, pack]
                left = from_west[group, pack]
                if part:
                    right = pltpu.roll(right, LANES - part * HALO, 1)
                if part + 1 < EDGES:
                    left = pltpu.roll(left, LANES - (part + 1) * HALO, 1)
                edge = jnp.where(lane < LANES // 2, right, left)
                west = jnp.where(
                    west_in,
                    jnp.take_along_axis(main, west_at, axis=1),
                    jnp.take_along_axis(edge, west_at, axis=1),
                )
                east = jnp.where(
                    east_in,
                    jnp.take_along_axis(main, east_at, axis=1),
                    jnp.take_along_axis(edge, east_at, axis=1),
                )
                values[t].append((1.0 - weight) * west + weight * east)
        coefs = [diffusion[level, at, :] for level in range(LEV - 1)]
        solved = solve_levels(values, coefs)
        for t in range(NTR):
            for level in range(LEV):
                rows[pl.ds(group * 8 * FEAT + level * NTR + t, 8, stride=FEAT), :] = solved[t][level]
        for spare in range(NTR * LEV, FEAT):
            rows[pl.ds(group * 8 * FEAT + spare, 8, stride=FEAT), :] = jnp.zeros((8, LANES), jnp.float32)
        return carry

    lax.fori_loop(0, groups, advect_group, 0)

    def turn(block, carry):
        at = pl.ds(pl.multiple_of(block * LANES, LANES), LANES)
        turned = rows[at, :].T
        for by in range(FOUR):
            table[by, at, :] = pltpu.roll(turned, by * FEAT, 1) if by else turned
        return carry

    lax.fori_loop(0, lat_rows // FOUR, turn, 0)

    table_rows = table.reshape(FOUR * lat_rows * LANES // FOUR, LANES)

    def send_step(step, carry):
        targets = []
        for member in range(FOUR):
            to_lon, to_lat = torus_target(lon, lat, (step // 2) * FOUR + member, step % 2)
            targets.append((to_lon, to_lat, to_lon * 2 + to_lat))
        for slot in range(LANES):
            for member in range(FOUR):
                at = address[targets[member][2], slot]
                stage[member, slot : slot + 1, :] = table_rows[pl.ds(at, 1), :]
        wide = stage[0]
        for member in range(1, FOUR):
            wide = jnp.where(lane_group == member, stage[member], wide)
        turned = wide.T
        for member in range(FOUR):
            to_lon, to_lat, owner = targets[member]
            box = step * FOUR + member
            outbox[box] = turned[member * FEAT : (member + 1) * FEAT, :]
            length = count[0, owner].astype(jnp.float32)
            outbox[box, SENT - 1 : SENT, :] = jnp.full((1, LANES), length, jnp.float32)
            slot = lax.rem(owner - me + PEERS, PEERS)

            def send():
                pltpu.make_async_remote_copy(
                    src_ref=outbox.at[box, 0:SENT], dst_ref=arrived.at[slot, 0:SENT],
                    send_sem=send_sem, recv_sem=recv_sem,
                    device_id=(to_lon, to_lat), device_id_type=MESH,
                ).start()

            if member:
                send()
            else:
                pl.when(step > 0)(send)
        return carry

    to_scalars.wait()
    lax.fori_loop(0, PEERS // FOUR, send_step, 0)
    arrived[0] = outbox[0]
    others = pltpu.make_async_copy(outbox.at[1:PEERS, 0:SENT], arrived.at[1:PEERS, 0:SENT], recv_sem)
    others.wait()
    pltpu.make_async_copy(outbox.at[1:PEERS, 0:SENT], arrived.at[1:PEERS, 0:SENT], send_sem).wait()
    lengths[...] = arrived[:, SENT - 1, :].T[0:1, :].astype(jnp.int32)


def place_kernel(arrived, lengths, out, owned):
    columns = out.shape[2]
    lane = lax.broadcasted_iota(jnp.int32, (FEAT, LANES), 1)

    def place(source, start):
        block = start // LANES
        shift = lax.rem(start, LANES)
        rolled = pltpu.roll(arrived[source], shift, 1)
        first = pl.ds(pl.multiple_of(block * FEAT, FEAT), FEAT)
        second = pl.ds(pl.multiple_of(block * FEAT + FEAT, FEAT), FEAT)
        pltpu.store(owned.at[first, :], rolled, mask=lane >= shift)
        owned[second, :] = rolled
        return start + lengths[0, source]

    lax.fori_loop(0, arrived.shape[0], place, jnp.int32(0), unroll=4)

    for block in range(columns // LANES):
        for level in range(LEV):
            begin = block * FEAT + level * NTR
            out[level, :, block * LANES : (block + 1) * LANES] = owned[begin : begin + NTR, :]


def body(tracers, offsets, weights, diffusion, send_index, send_count):
    lat_rows, lon_width = tracers.shape[2:]
    columns = lat_rows * lon_width
    groups = lat_rows // 8
    packs = -(-NTR * LEV // EDGES)
    vmem = pl.BlockSpec(memory_space=pltpu.VMEM)
    smem = pl.BlockSpec(memory_space=pltpu.SMEM)
    edge = pltpu.VMEM((groups, packs, 8, LANES), jnp.float32)
    arrived, lengths = pl.pallas_call(
        exchange_kernel,
        out_shape=(
            jax.ShapeDtypeStruct((PEERS, FEAT, LANES), jnp.float32),
            jax.ShapeDtypeStruct((1, PEERS), jnp.int32),
        ),
        in_specs=[vmem] * 5 + [smem],
        out_specs=(vmem, vmem),
        scratch_shapes=[
            edge, edge, edge, edge,
            pltpu.VMEM((lat_rows * FEAT, LANES), jnp.float32),
            pltpu.VMEM((FOUR, columns // FOUR, LANES), jnp.float32),
            pltpu.VMEM((FOUR, LANES, LANES), jnp.float32),
            pltpu.VMEM((PEERS, FEAT, LANES), jnp.float32),
            pltpu.VMEM((PEERS, LANES), jnp.int32),
            pltpu.SMEM((PEERS, LANES), jnp.int32),
            pltpu.SemaphoreType.DMA((4,)),
            pltpu.SemaphoreType.DMA,
            pltpu.SemaphoreType.DMA,
            pltpu.SemaphoreType.DMA,
        ],
        compiler_params=pltpu.CompilerParams(vmem_limit_bytes=40 << 20, collective_id=0, has_side_effects=True),
        name="advect_solve_exchange",
    )(tracers, offsets, weights, diffusion, send_index[0], send_count)
    owned = pl.pallas_call(
        place_kernel,
        out_shape=jax.ShapeDtypeStruct((LEV, NTR, columns), jnp.float32),
        in_specs=[vmem, smem],
        out_specs=vmem,
        scratch_shapes=[pltpu.VMEM(((columns // LANES + 2) * FEAT, LANES), jnp.float32)],
        compiler_params=pltpu.CompilerParams(vmem_limit_bytes=32 << 20),
        name="place_owned",
    )(arrived, lengths)
    return jnp.transpose(owned, (1, 0, 2))


def solution(mesh):
    return jax.shard_map(
        body,
        mesh=mesh,
        in_specs=(
            P(None, None, "lat", "lon"),
            P(None, "lat", "lon"),
            P(None, "lat", "lon"),
            P(None, "lat", "lon"),
            P(("lon", "lat"), None, None),
            P(("lon", "lat"), None),
        ),
        out_specs=P(None, None, ("lon", "lat")),
        check_vma=False,
    )
```

```python
import jax
import jax.numpy as jnp
from jax import lax
from jax.experimental import pallas as pl
from jax.experimental.pallas import tpu as pltpu
from jax.sharding import PartitionSpec as P

NTR = 3
LEV = 10
HALO = 16
FEAT = 32
SENT = NTR * LEV + 1
LANES = 128
FOUR = LANES // FEAT
EDGES = LANES // HALO
PEERS = 128
ROW = 16
AXES = ("lon", "lat")
MESH = pl.DeviceIdType.MESH


def torus_target(lon, lat, shift, flip):
    x, y, z, core = (lon // 8) % 4, lat * 2 + lon // 32, (lon // 2) % 4, lon % 2
    x = (x + shift) % 4
    y = (y + shift // 4 + shift) % 4
    z = (z + shift // 16 + shift // 4 + shift) % 4
    core = (core + flip) % 2
    return (y % 2) * 32 + x * 8 + z * 2 + core, y // 2


def factor_levels(coefs):
    inverses, uppers = [], []
    for level in range(LEV):
        denom = jnp.ones_like(coefs[0])
        if level > 0:
            denom = denom + coefs[level - 1]
        if level < LEV - 1:
            denom = denom + coefs[level]
        if level > 0:
            denom = denom - coefs[level - 1] * uppers[level - 1]
        inverses.append(1.0 / denom)
        if level < LEV - 1:
            uppers.append(coefs[level] * inverses[level])
    return inverses, uppers


def solve_levels(values, coefs, inverses, uppers):
    reduced = []
    for level in range(LEV):
        right = values[level]
        if level > 0:
            right = right + coefs[level - 1] * reduced[level - 1]
        reduced.append(right * inverses[level])
    output = [None] * LEV
    output[LEV - 1] = reduced[LEV - 1]
    for level in range(LEV - 2, -1, -1):
        output[level] = reduced[level] + uppers[level] * output[level + 1]
    return output


def exchange_kernel(
    tracers_hbm, offsets_hbm, weights_hbm, diffusion_hbm, index_hbm, count_hbm, arrived, lengths,
    tracers, offsets, weights, diffusion, index, count, partial, factors,
    edge_low, edge_high, from_east, from_west, rows, table, stage, outbox, place, address,
    load_sems, edge_sems, address_sem, send_sem, recv_sem, ready,
):
    pairs = (
        (tracers_hbm, tracers), (index_hbm, index), (offsets_hbm, offsets),
        (weights_hbm, weights), (diffusion_hbm, diffusion), (count_hbm, count),
    )
    loads = [pltpu.make_async_copy(source, here, load_sems.at[i]) for i, (source, here) in enumerate(pairs)]
    for load in loads:
        load.start()
    lat_rows = tracers.shape[2]
    groups = lat_rows // 8
    packs = from_east.shape[1]
    lon, lat = lax.axis_index("lon"), lax.axis_index("lat")
    bands = lax.axis_size("lon")
    me = lon * 2 + lat
    lane = lax.broadcasted_iota(jnp.int32, (8, LANES), 1)
    lane_group = lax.broadcasted_iota(jnp.int32, (LANES, LANES), 1) // FEAT

    barrier = pltpu.get_barrier_semaphore()

    row_first, in_row = (me // ROW) * ROW, lax.rem(me, ROW)

    def greet(semaphore, other):
        pl.semaphore_signal(semaphore, inc=1, device_id=(other // 2, lax.rem(other, 2)), device_id_type=MESH)

    for ring in (2, PEERS - 2):
        greet(barrier, lax.rem(me + ring, PEERS))
    for step in range(1, ROW):
        greet(barrier, row_first + lax.rem(in_row + step, ROW))
    for step in range(ROW, PEERS, ROW):
        greet(barrier, lax.rem(me + step, PEERS))

    loads[0].wait()

    def pack_edges(group, carry):
        at = pl.ds(pl.multiple_of(group * 8, 8), 8)
        for pack in range(packs):
            low = high = None
            for part in range(EDGES):
                plane = pack * EDGES + part
                if plane >= NTR * LEV:
                    continue
                value = tracers[plane // LEV, plane % LEV, at, :]
                low_at = (part + EDGES // 2) % EDGES
                to_low = pltpu.roll(value, low_at * HALO, 1) if low_at else value
                to_high = pltpu.roll(value, (part + 1) * HALO, 1) if part + 1 < EDGES else value
                low = to_low if part == 0 else jnp.where(lane // HALO == low_at, to_low, low)
                high = to_high if part == 0 else jnp.where(lane // HALO == part, to_high, high)
            edge_low[group, pack] = low
            edge_high[group, pack] = high
        return carry

    lax.fori_loop(0, groups, pack_edges, 0)

    pl.semaphore_wait(barrier, 2 + ROW - 1 + PEERS // ROW - 1)
    to_west = pltpu.make_async_remote_copy(
        src_ref=edge_low, dst_ref=from_east, send_sem=edge_sems.at[0], recv_sem=edge_sems.at[1],
        device_id=(lax.rem(lon + bands - 1, bands), lat), device_id_type=MESH,
    )
    to_east = pltpu.make_async_remote_copy(
        src_ref=edge_high, dst_ref=from_west, send_sem=edge_sems.at[2], recv_sem=edge_sems.at[3],
        device_id=(lax.rem(lon + 1, bands), lat), device_id_type=MESH,
    )
    to_west.start()
    to_east.start()
    for step in range(1, ROW):
        greet(ready, row_first + lax.rem(in_row + step, ROW))

    loads[1].wait()
    column = index[...]
    owner = lax.broadcasted_iota(jnp.int32, column.shape, 0)
    member_of = ((owner // 16) % 4 - (lon // 8) % 4 + 4) % 4
    row = column // LANES
    turn_by = (member_of - row % 4 + 4) % 4
    place[...] = turn_by * (lat_rows * LANES // 4) + (row // 4) * LANES + column % LANES
    to_scalars = pltpu.make_async_copy(place, address, address_sem)
    to_scalars.start()

    for load in loads[2:]:
        load.wait()

    def interior(group, carry):
        at = pl.ds(pl.multiple_of(group * 8, 8), 8)
        for level in range(LEV):
            cell = lane + offsets[level, at, :]
            weight = weights[level, at, :]
            west_weight = jnp.where((cell >= 0) & (cell < LANES), 1.0 - weight, 0.0)
            east_weight = jnp.where((cell >= -1) & (cell < LANES - 1), weight, 0.0)
            west_at = cell & (LANES - 1)
            east_at = (cell + 1) & (LANES - 1)
            for t in range(NTR):
                main = tracers[t, level, at, :]
                west = jnp.take_along_axis(main, west_at, axis=1)
                east = jnp.take_along_axis(main, east_at, axis=1)
                partial[t, level, at, :] = west_weight * west + east_weight * east
        inverses, uppers = factor_levels([diffusion[level, at, :] for level in range(LEV - 1)])
        for level in range(LEV):
            factors[level, at, :] = inverses[level]
        for level in range(LEV - 1):
            factors[LEV + level, at, :] = uppers[level]
        return carry

    lax.fori_loop(0, groups, interior, 0)
    to_west.wait()
    to_east.wait()

    def finish(group, carry):
        at = pl.ds(pl.multiple_of(group * 8, 8), 8)
        values = [[None] * LEV for _ in range(NTR)]
        for level in range(LEV):
            cell = lane + offsets[level, at, :]
            weight = weights[level, at, :]
            west_weight = jnp.where((cell >= 0) & (cell < LANES), 0.0, 1.0 - weight)
            east_weight = jnp.where((cell >= -1) & (cell < LANES - 1), 0.0, weight)
            west_at = (cell & (HALO - 1)) + jnp.where(cell < 0, 0, LANES // 2)
            east_at = ((cell + 1) & (HALO - 1)) + jnp.where(cell < -1, 0, LANES // 2)
            for t in range(NTR):
                plane = t * LEV + level
                pack, part = plane // EDGES, plane % EDGES
                edge = jnp.where(lane // HALO == part, from_west[group, pack], from_east[group, pack])
                west = jnp.take_along_axis(edge, (west_at + part * HALO) & (LANES - 1), axis=1)
                east = jnp.take_along_axis(edge, (east_at + part * HALO) & (LANES - 1), axis=1)
                values[t][level] = partial[t, level, at, :] + (west_weight * west + east_weight * east)
        coefs = [diffusion[level, at, :] for level in range(LEV - 1)]
        inverses = [factors[level, at, :] for level in range(LEV)]
        uppers = [factors[LEV + level, at, :] for level in range(LEV - 1)]
        for t in range(NTR):
            solved = solve_levels(values[t], coefs, inverses, uppers)
            for level in range(LEV):
                rows[pl.ds(group * 8 * FEAT + level * NTR + t, 8, stride=FEAT), :] = solved[level]
        for spare in range(NTR * LEV, FEAT):
            rows[pl.ds(group * 8 * FEAT + spare, 8, stride=FEAT), :] = jnp.zeros((8, LANES), jnp.float32)
        return carry

    lax.fori_loop(0, groups, finish, 0)

    def turn(block, carry):
        at = pl.ds(pl.multiple_of(block * LANES, LANES), LANES)
        turned = rows[at, :].T
        for by in range(FOUR):
            table[by, at, :] = pltpu.roll(turned, by * FEAT, 1) if by else turned
        return carry

    lax.fori_loop(0, lat_rows // FOUR, turn, 0)

    table_rows = table.reshape(FOUR * lat_rows * LANES // FOUR, LANES)

    def send_step(step, carry):
        targets = []
        for member in range(FOUR):
            to_lon, to_lat = torus_target(lon, lat, (step // 2) * FOUR + member, step % 2)
            targets.append((to_lon, to_lat, to_lon * 2 + to_lat))
        for slot in range(LANES):
            for member in range(FOUR):
                at = address[targets[member][2], slot]
                stage[member, slot : slot + 1, :] = table_rows[pl.ds(at, 1), :]
        wide = stage[0]
        for member in range(1, FOUR):
            wide = jnp.where(lane_group == member, stage[member], wide)
        turned = wide.T
        for member in range(FOUR):
            to_lon, to_lat, owner = targets[member]
            box = step * FOUR + member
            outbox[box] = turned[member * FEAT : (member + 1) * FEAT, :]
            length = count[0, owner].astype(jnp.float32)
            outbox[box, SENT - 1 : SENT, :] = jnp.full((1, LANES), length, jnp.float32)
            slot = lax.rem(owner - me + PEERS, PEERS)

            def send():
                pltpu.make_async_remote_copy(
                    src_ref=outbox.at[box, 0:SENT], dst_ref=arrived.at[slot, 0:SENT],
                    send_sem=send_sem, recv_sem=recv_sem,
                    device_id=(to_lon, to_lat), device_id_type=MESH,
                ).start()

            if member:
                send()
            else:
                pl.when(step > 0)(send)
        return carry

    to_scalars.wait()
    pl.semaphore_wait(ready, ROW - 1)
    lax.fori_loop(0, PEERS // FOUR, send_step, 0)
    arrived[0] = outbox[0]
    others = pltpu.make_async_copy(outbox.at[1:PEERS, 0:SENT], arrived.at[1:PEERS, 0:SENT], recv_sem)
    others.wait()
    pltpu.make_async_copy(outbox.at[1:PEERS, 0:SENT], arrived.at[1:PEERS, 0:SENT], send_sem).wait()
    lengths[...] = arrived[:, SENT - 1, :].T[0:1, :].astype(jnp.int32)


def place_kernel(arrived, lengths, out, owned):
    columns = out.shape[2]
    lane = lax.broadcasted_iota(jnp.int32, (FEAT, LANES), 1)

    def place(source, start):
        block = start // LANES
        shift = lax.rem(start, LANES)
        rolled = pltpu.roll(arrived[source], shift, 1)
        first = pl.ds(pl.multiple_of(block * FEAT, FEAT), FEAT)
        second = pl.ds(pl.multiple_of(block * FEAT + FEAT, FEAT), FEAT)
        pltpu.store(owned.at[first, :], rolled, mask=lane >= shift)
        owned[second, :] = rolled
        return start + lengths[0, source]

    lax.fori_loop(0, arrived.shape[0], place, jnp.int32(0), unroll=4)

    for block in range(columns // LANES):
        for level in range(LEV):
            begin = block * FEAT + level * NTR
            out[level, :, block * LANES : (block + 1) * LANES] = owned[begin : begin + NTR, :]


def body(tracers, offsets, weights, diffusion, send_index, send_count):
    lat_rows, lon_width = tracers.shape[2:]
    columns = lat_rows * lon_width
    groups = lat_rows // 8
    packs = -(-NTR * LEV // EDGES)
    vmem = pl.BlockSpec(memory_space=pltpu.VMEM)
    smem = pl.BlockSpec(memory_space=pltpu.SMEM)
    edge = pltpu.VMEM((groups, packs, 8, LANES), jnp.float32)
    arrived, lengths = pl.pallas_call(
        exchange_kernel,
        out_shape=(
            jax.ShapeDtypeStruct((PEERS, FEAT, LANES), jnp.float32),
            jax.ShapeDtypeStruct((1, PEERS), jnp.int32),
        ),
        in_specs=[pl.BlockSpec(memory_space=pltpu.HBM)] * 6,
        out_specs=(vmem, vmem),
        scratch_shapes=[
            pltpu.VMEM(tracers.shape, jnp.float32),
            pltpu.VMEM(offsets.shape, jnp.int32),
            pltpu.VMEM(weights.shape, jnp.float32),
            pltpu.VMEM(diffusion.shape, jnp.float32),
            pltpu.VMEM((PEERS, LANES), jnp.int32),
            pltpu.SMEM((1, PEERS), jnp.int32),
            pltpu.VMEM(tracers.shape, jnp.float32),
            pltpu.VMEM((2 * LEV - 1, lat_rows, lon_width), jnp.float32),
            edge, edge, edge, edge,
            pltpu.VMEM((lat_rows * FEAT, LANES), jnp.float32),
            pltpu.VMEM((FOUR, columns // FOUR, LANES), jnp.float32),
            pltpu.VMEM((FOUR, LANES, LANES), jnp.float32),
            pltpu.VMEM((PEERS, FEAT, LANES), jnp.float32),
            pltpu.VMEM((PEERS, LANES), jnp.int32),
            pltpu.SMEM((PEERS, LANES), jnp.int32),
            pltpu.SemaphoreType.DMA((6,)),
            pltpu.SemaphoreType.DMA((4,)),
            pltpu.SemaphoreType.DMA,
            pltpu.SemaphoreType.DMA,
            pltpu.SemaphoreType.DMA,
            pltpu.SemaphoreType.REGULAR,
        ],
        compiler_params=pltpu.CompilerParams(vmem_limit_bytes=66800000, collective_id=0, has_side_effects=True),
        name="advect_solve_exchange",
    )(tracers, offsets, weights, diffusion, send_index[0], send_count)
    owned = pl.pallas_call(
        place_kernel,
        out_shape=jax.ShapeDtypeStruct((LEV, NTR, columns), jnp.float32),
        in_specs=[vmem, smem],
        out_specs=vmem,
        scratch_shapes=[pltpu.VMEM(((columns // LANES + 2) * FEAT, LANES), jnp.float32)],
        compiler_params=pltpu.CompilerParams(vmem_limit_bytes=32 << 20),
        name="place_owned",
    )(arrived, lengths)
    return jnp.transpose(owned, (1, 0, 2))


def solution(mesh):
    return jax.shard_map(
        body,
        mesh=mesh,
        in_specs=(
            P(None, None, "lat", "lon"),
            P(None, "lat", "lon"),
            P(None, "lat", "lon"),
            P(None, "lat", "lon"),
            P(("lon", "lat"), None, None),
            P(("lon", "lat"), None),
        ),
        out_specs=P(None, None, ("lon", "lat")),
        check_vma=False,
    )
```

```python
import jax
import jax.numpy as jnp
from jax import lax
from jax.experimental import pallas as pl
from jax.experimental.pallas import tpu as pltpu
from jax.sharding import PartitionSpec as P

NTR = 3
LEV = 10
HALO = 16
FEAT = 32
SENT = NTR * LEV + 1
LANES = 128
FOUR = LANES // FEAT
EDGES = LANES // HALO
PEERS = 128
ROW = 16
PIECE = 2
OUT_PIECES = 4
AXES = ("lon", "lat")
MESH = pl.DeviceIdType.MESH


def torus_target(lon, lat, shift, flip):
    x, y, z, core = (lon // 8) % 4, lat * 2 + lon // 32, (lon // 2) % 4, lon % 2
    x = (x + shift) % 4
    y = (y + shift // 4 + shift) % 4
    z = (z + shift // 16 + shift // 4 + shift) % 4
    core = (core + flip) % 2
    return (y % 2) * 32 + x * 8 + z * 2 + core, y // 2


def factor_levels(coefs):
    inverses, uppers = [], []
    for level in range(LEV):
        denom = jnp.ones_like(coefs[0])
        if level > 0:
            denom = denom + coefs[level - 1]
        if level < LEV - 1:
            denom = denom + coefs[level]
        if level > 0:
            denom = denom - coefs[level - 1] * uppers[level - 1]
        inverses.append(1.0 / denom)
        if level < LEV - 1:
            uppers.append(coefs[level] * inverses[level])
    return inverses, uppers


def solve_levels(values, coefs, inverses, uppers):
    reduced = []
    for level in range(LEV):
        right = values[level]
        if level > 0:
            right = right + coefs[level - 1] * reduced[level - 1]
        reduced.append(right * inverses[level])
    output = [None] * LEV
    output[LEV - 1] = reduced[LEV - 1]
    for level in range(LEV - 2, -1, -1):
        output[level] = reduced[level] + uppers[level] * output[level + 1]
    return output


def exchange_kernel(
    tracers_hbm, offsets_hbm, weights_hbm, diffusion_hbm, index_hbm, count_hbm, arrived, lengths,
    tracers, offsets, weights, diffusion, index, count, partial, factors,
    edge_low, edge_high, from_east, from_west, rows, table, stage, outbox, place, address,
    load_sems, edge_sems, address_sem, send_sem, recv_sem, ready,
):
    pairs = (
        (tracers_hbm, tracers), (index_hbm, index), (offsets_hbm, offsets),
        (weights_hbm, weights), (diffusion_hbm, diffusion), (count_hbm, count),
    )
    loads = [pltpu.make_async_copy(source, here, load_sems.at[i]) for i, (source, here) in enumerate(pairs)]
    for load in loads:
        load.start()
    lat_rows = tracers.shape[2]
    groups = lat_rows // 8
    packs = from_east.shape[1]
    lon, lat = lax.axis_index("lon"), lax.axis_index("lat")
    bands = lax.axis_size("lon")
    me = lon * 2 + lat
    lane = lax.broadcasted_iota(jnp.int32, (8, LANES), 1)
    lane_group = lax.broadcasted_iota(jnp.int32, (LANES, LANES), 1) // FEAT

    barrier = pltpu.get_barrier_semaphore()

    row_first, in_row = (me // ROW) * ROW, lax.rem(me, ROW)

    def greet(semaphore, other):
        pl.semaphore_signal(semaphore, inc=1, device_id=(other // 2, lax.rem(other, 2)), device_id_type=MESH)

    for ring in (2, PEERS - 2):
        greet(barrier, lax.rem(me + ring, PEERS))
    for step in range(1, ROW):
        greet(barrier, row_first + lax.rem(in_row + step, ROW))
    for step in range(ROW, PEERS, ROW):
        greet(barrier, lax.rem(me + step, PEERS))

    loads[0].wait()

    def pack_edges(group, carry):
        at = pl.ds(pl.multiple_of(group * 8, 8), 8)
        for pack in range(packs):
            low = high = None
            for part in range(EDGES):
                plane = pack * EDGES + part
                if plane >= NTR * LEV:
                    continue
                value = tracers[plane // LEV, plane % LEV, at, :]
                low_at = (part + EDGES // 2) % EDGES
                to_low = pltpu.roll(value, low_at * HALO, 1) if low_at else value
                to_high = pltpu.roll(value, (part + 1) * HALO, 1) if part + 1 < EDGES else value
                low = to_low if part == 0 else jnp.where(lane // HALO == low_at, to_low, low)
                high = to_high if part == 0 else jnp.where(lane // HALO == part, to_high, high)
            edge_low[group, pack] = low
            edge_high[group, pack] = high
        return carry

    def edge_copies(piece):
        part = pl.ds(piece * PIECE, PIECE)
        return [
            pltpu.make_async_remote_copy(
                src_ref=source.at[part], dst_ref=target.at[part],
                send_sem=edge_sems.at[side, 0, piece], recv_sem=edge_sems.at[side, 1, piece],
                device_id=(lax.rem(lon + distance, bands), lat), device_id_type=MESH,
            )
            for side, source, target, distance in ((0, edge_low, from_east, bands - 1), (1, edge_high, from_west, 1))
        ]

    pieces = groups // PIECE
    for piece in range(pieces):
        lax.fori_loop(piece * PIECE, piece * PIECE + PIECE, pack_edges, 0, unroll=True)
        if piece == 0:
            pl.semaphore_wait(barrier, 2 + ROW - 1 + PEERS // ROW - 1)
        for copy in edge_copies(piece):
            copy.start()
    for step in range(1, ROW):
        greet(ready, row_first + lax.rem(in_row + step, ROW))

    loads[1].wait()
    column = index[...]
    owner = lax.broadcasted_iota(jnp.int32, column.shape, 0)
    member_of = ((owner // 16) % 4 - (lon // 8) % 4 + 4) % 4
    row = column // LANES
    turn_by = (member_of - row % 4 + 4) % 4
    place[...] = turn_by * (lat_rows * LANES // 4) + (row // 4) * LANES + column % LANES
    to_scalars = pltpu.make_async_copy(place, address, address_sem)
    to_scalars.start()

    for load in loads[2:]:
        load.wait()

    def interior(group, carry):
        at = pl.ds(pl.multiple_of(group * 8, 8), 8)
        for level in range(LEV):
            cell = lane + offsets[level, at, :]
            weight = weights[level, at, :]
            west_weight = jnp.where((cell >= 0) & (cell < LANES), 1.0 - weight, 0.0)
            east_weight = jnp.where((cell >= -1) & (cell < LANES - 1), weight, 0.0)
            west_at = cell & (LANES - 1)
            east_at = (cell + 1) & (LANES - 1)
            for t in range(NTR):
                main = tracers[t, level, at, :]
                west = jnp.take_along_axis(main, west_at, axis=1)
                east = jnp.take_along_axis(main, east_at, axis=1)
                partial[t, level, at, :] = west_weight * west + east_weight * east
        inverses, uppers = factor_levels([diffusion[level, at, :] for level in range(LEV - 1)])
        for level in range(LEV):
            factors[level, at, :] = inverses[level]
        for level in range(LEV - 1):
            factors[LEV + level, at, :] = uppers[level]
        return carry

    lax.fori_loop(0, groups, interior, 0)

    def finish(group, carry):
        at = pl.ds(pl.multiple_of(group * 8, 8), 8)
        values = [[None] * LEV for _ in range(NTR)]
        for level in range(LEV):
            cell = lane + offsets[level, at, :]
            weight = weights[level, at, :]
            west_weight = jnp.where((cell >= 0) & (cell < LANES), 0.0, 1.0 - weight)
            east_weight = jnp.where((cell >= -1) & (cell < LANES - 1), 0.0, weight)
            west_at = (cell & (HALO - 1)) + jnp.where(cell < 0, 0, LANES // 2)
            east_at = ((cell + 1) & (HALO - 1)) + jnp.where(cell < -1, 0, LANES // 2)
            for t in range(NTR):
                plane = t * LEV + level
                pack, part = plane // EDGES, plane % EDGES
                edge = jnp.where(lane // HALO == part, from_west[group, pack], from_east[group, pack])
                west = jnp.take_along_axis(edge, (west_at + part * HALO) & (LANES - 1), axis=1)
                east = jnp.take_along_axis(edge, (east_at + part * HALO) & (LANES - 1), axis=1)
                values[t][level] = partial[t, level, at, :] + (west_weight * west + east_weight * east)
        coefs = [diffusion[level, at, :] for level in range(LEV - 1)]
        inverses = [factors[level, at, :] for level in range(LEV)]
        uppers = [factors[LEV + level, at, :] for level in range(LEV - 1)]
        for t in range(NTR):
            solved = solve_levels(values[t], coefs, inverses, uppers)
            for level in range(LEV):
                rows[pl.ds(group * 8 * FEAT + level * NTR + t, 8, stride=FEAT), :] = solved[level]
        for spare in range(NTR * LEV, FEAT):
            rows[pl.ds(group * 8 * FEAT + spare, 8, stride=FEAT), :] = jnp.zeros((8, LANES), jnp.float32)
        return carry

    def turn(block, carry):
        at = pl.ds(pl.multiple_of(block * LANES, LANES), LANES)
        turned = rows[at, :].T
        for by in range(FOUR):
            table[by, at, :] = pltpu.roll(turned, by * FEAT, 1) if by else turned
        return carry

    def finish_piece(piece, carry):
        for copy in edge_copies(piece):
            copy.wait_recv()
        lax.fori_loop(piece * PIECE, piece * PIECE + PIECE, finish, 0)
        blocks = PIECE * 8 // FOUR
        for block in range(blocks):
            turn(piece * blocks + block, 0)
        return carry

    lax.fori_loop(0, pieces, finish_piece, 0)

    table_rows = table.reshape(FOUR * lat_rows * LANES // FOUR, LANES)

    def targets_of(step):
        targets = []
        for member in range(FOUR):
            to_lon, to_lat = torus_target(lon, lat, (step // 2) * FOUR + member, step % 2)
            targets.append((to_lon, to_lat, to_lon * 2 + to_lat))
        return targets

    def gather(step, half):
        owners = [owner for _, _, owner in targets_of(step)]
        for slot in range(LANES):
            for member in range(FOUR):
                at = address[owners[member], slot]
                stage[half, member, slot : slot + 1, :] = table_rows[pl.ds(at, 1), :]

    def send(step, half, first=0):
        wide = stage[half, 0]
        for member in range(1, FOUR):
            wide = jnp.where(lane_group == member, stage[half, member], wide)
        turned = wide.T
        for member, (to_lon, to_lat, owner) in enumerate(targets_of(step)):
            box = step * FOUR + member
            outbox[box] = turned[member * FEAT : (member + 1) * FEAT, :]
            length = count[0, owner].astype(jnp.float32)
            outbox[box, SENT - 1 : SENT, :] = jnp.full((1, LANES), length, jnp.float32)
            slot = lax.rem(owner - me + PEERS, PEERS)
            if member >= first:
                pltpu.make_async_remote_copy(
                    src_ref=outbox.at[box, 0:SENT], dst_ref=arrived.at[slot, 0:SENT],
                    send_sem=send_sem, recv_sem=recv_sem,
                    device_id=(to_lon, to_lat), device_id_type=MESH,
                ).start()

    to_scalars.wait()
    pl.semaphore_wait(ready, ROW - 1)
    steps = PEERS // FOUR
    gather(0, 0)
    send(0, 0, first=1)
    gather(1, 1)

    def two_steps(turn_at, carry):
        send(2 * turn_at + 1, 1)
        gather(2 * turn_at + 2, 0)
        send(2 * turn_at + 2, 0)
        gather(2 * turn_at + 3, 1)
        return carry

    lax.fori_loop(0, steps // 2 - 1, two_steps, 0)
    send(steps - 1, 1)
    arrived[0] = outbox[0]
    others = pltpu.make_async_copy(outbox.at[1:PEERS, 0:SENT], arrived.at[1:PEERS, 0:SENT], recv_sem)
    others.wait()
    pltpu.make_async_copy(outbox.at[1:PEERS, 0:SENT], arrived.at[1:PEERS, 0:SENT], send_sem).wait()
    lengths[...] = arrived[:, SENT - 1, :].T[0:1, :].astype(jnp.int32)
    for piece in range(pieces):
        for copy in edge_copies(piece):
            copy.wait_send()


def place_kernel(arrived, lengths, out, owned, rows, out_sems):
    columns = out.shape[2]
    lane = lax.broadcasted_iota(jnp.int32, (FEAT, LANES), 1)

    def place(source, start):
        block = start // LANES
        shift = lax.rem(start, LANES)
        rolled = pltpu.roll(arrived[source], shift, 1)
        first = pl.ds(pl.multiple_of(block * FEAT, FEAT), FEAT)
        second = pl.ds(pl.multiple_of(block * FEAT + FEAT, FEAT), FEAT)
        pltpu.store(owned.at[first, :], rolled, mask=lane >= shift)
        owned[second, :] = rolled
        return start + lengths[0, source]

    lax.fori_loop(0, arrived.shape[0], place, jnp.int32(0), unroll=16)

    copies = []
    width = columns // OUT_PIECES
    for piece in range(OUT_PIECES):
        for block in range(piece * width // LANES, (piece + 1) * width // LANES):
            for level in range(LEV):
                begin = block * FEAT + level * NTR
                rows[level, :, block * LANES : (block + 1) * LANES] = owned[begin : begin + NTR, :]
        part = pl.ds(piece * width, width)
        copies.append(pltpu.make_async_copy(rows.at[:, :, part], out.at[:, :, part], out_sems.at[piece]))
        copies[-1].start()
    for copy in copies:
        copy.wait()


def body(tracers, offsets, weights, diffusion, send_index, send_count):
    lat_rows, lon_width = tracers.shape[2:]
    columns = lat_rows * lon_width
    groups = lat_rows // 8
    packs = -(-NTR * LEV // EDGES)
    vmem = pl.BlockSpec(memory_space=pltpu.VMEM)
    smem = pl.BlockSpec(memory_space=pltpu.SMEM)
    edge = pltpu.VMEM((groups, packs, 8, LANES), jnp.float32)
    arrived, lengths = pl.pallas_call(
        exchange_kernel,
        out_shape=(
            jax.ShapeDtypeStruct((PEERS, FEAT, LANES), jnp.float32),
            jax.ShapeDtypeStruct((1, PEERS), jnp.int32),
        ),
        in_specs=[pl.BlockSpec(memory_space=pltpu.HBM)] * 6,
        out_specs=(vmem, vmem),
        scratch_shapes=[
            pltpu.VMEM(tracers.shape, jnp.float32),
            pltpu.VMEM(offsets.shape, jnp.int32),
            pltpu.VMEM(weights.shape, jnp.float32),
            pltpu.VMEM(diffusion.shape, jnp.float32),
            pltpu.VMEM((PEERS, LANES), jnp.int32),
            pltpu.SMEM((1, PEERS), jnp.int32),
            pltpu.VMEM(tracers.shape, jnp.float32),
            pltpu.VMEM((2 * LEV - 1, lat_rows, lon_width), jnp.float32),
            edge, edge, edge, edge,
            pltpu.VMEM((lat_rows * FEAT, LANES), jnp.float32),
            pltpu.VMEM((FOUR, columns // FOUR, LANES), jnp.float32),
            pltpu.VMEM((2, FOUR, LANES, LANES), jnp.float32),
            pltpu.VMEM((PEERS, FEAT, LANES), jnp.float32),
            pltpu.VMEM((PEERS, LANES), jnp.int32),
            pltpu.SMEM((PEERS, LANES), jnp.int32),
            pltpu.SemaphoreType.DMA((6,)),
            pltpu.SemaphoreType.DMA((2, 2, groups // PIECE)),
            pltpu.SemaphoreType.DMA,
            pltpu.SemaphoreType.DMA,
            pltpu.SemaphoreType.DMA,
            pltpu.SemaphoreType.REGULAR,
        ],
        compiler_params=pltpu.CompilerParams(vmem_limit_bytes=40 << 20, collective_id=0, has_side_effects=True),
        name="advect_solve_exchange",
    )(*(pltpu.with_memory_space_constraint(x, pltpu.HBM) for x in (tracers, offsets, weights, diffusion, send_index[0], send_count)))
    owned = pl.pallas_call(
        place_kernel,
        out_shape=jax.ShapeDtypeStruct((LEV, NTR, columns), jnp.float32),
        in_specs=[vmem, smem],
        out_specs=pl.BlockSpec(memory_space=pltpu.HBM),
        scratch_shapes=[
            pltpu.VMEM(((columns // LANES + 2) * FEAT, LANES), jnp.float32),
            pltpu.VMEM((LEV, NTR, columns), jnp.float32),
            pltpu.SemaphoreType.DMA((OUT_PIECES,)),
        ],
        compiler_params=pltpu.CompilerParams(vmem_limit_bytes=32 << 20),
        name="place_owned",
    )(arrived, lengths)
    return jnp.transpose(owned, (1, 0, 2))


def solution(mesh):
    return jax.shard_map(
        body,
        mesh=mesh,
        in_specs=(
            P(None, None, "lat", "lon"),
            P(None, "lat", "lon"),
            P(None, "lat", "lon"),
            P(None, "lat", "lon"),
            P(("lon", "lat"), None, None),
            P(("lon", "lat"), None),
        ),
        out_specs=P(None, None, ("lon", "lat")),
        check_vma=False,
    )
```

```python
import jax
import jax.numpy as jnp
from jax import lax
from jax.experimental import pallas as pl
from jax.experimental.pallas import tpu as pltpu
from jax.sharding import PartitionSpec as P

NTR = 3
LEV = 10
HALO = 16
FEAT = 32
SENT = NTR * LEV + 1
LANES = 128
FOUR = LANES // FEAT
EDGES = LANES // HALO
PEERS = 128
PIECE = 2
OUT_PIECES = 4
AXES = ("lon", "lat")
MESH = pl.DeviceIdType.MESH


def factor_levels(coefs):
    inverses, uppers = [], []
    for level in range(LEV):
        denom = jnp.ones_like(coefs[0])
        if level > 0:
            denom = denom + coefs[level - 1]
        if level < LEV - 1:
            denom = denom + coefs[level]
        if level > 0:
            denom = denom - coefs[level - 1] * uppers[level - 1]
        inverses.append(1.0 / denom)
        if level < LEV - 1:
            uppers.append(coefs[level] * inverses[level])
    return inverses, uppers


def solve_levels(values, coefs, inverses, uppers):
    reduced = []
    for level in range(LEV):
        right = values[level]
        if level > 0:
            right = right + coefs[level - 1] * reduced[level - 1]
        reduced.append(right * inverses[level])
    output = [None] * LEV
    output[LEV - 1] = reduced[LEV - 1]
    for level in range(LEV - 2, -1, -1):
        output[level] = reduced[level] + uppers[level] * output[level + 1]
    return output


def exchange_kernel(
    tracers_hbm, offsets_hbm, weights_hbm, diffusion_hbm, index_hbm, count_hbm, arrived, lengths,
    tracers, offsets, weights, diffusion, index, count, partial, factors,
    edge_low, edge_high, from_east, from_west, rows, table, stage, outbox, place, address,
    load_sems, edge_sems, address_sem, send_sem, recv_sem, ready,
):
    pairs = (
        (tracers_hbm, tracers), (index_hbm, index), (offsets_hbm, offsets),
        (weights_hbm, weights), (diffusion_hbm, diffusion), (count_hbm, count),
    )
    loads = [pltpu.make_async_copy(source, here, load_sems.at[i]) for i, (source, here) in enumerate(pairs)]
    loads[0].start()
    lat_rows = tracers.shape[2]
    groups = lat_rows // 8
    packs = from_east.shape[1]
    lon, lat = lax.axis_index("lon"), lax.axis_index("lat")
    bands = lax.axis_size("lon")
    me = lon * 2 + lat
    lane = lax.broadcasted_iota(jnp.int32, (8, LANES), 1)
    sublanes = lax.broadcasted_iota(jnp.int32, (8, LANES), 0)

    barrier = pltpu.get_barrier_semaphore()

    def digit_mates(low, span):
        mask = span - low
        return [(me & (PEERS - 1 - mask)) + ((me + low * step) & mask) for step in range(1, span // low)]

    def greet(semaphore, other):
        pl.semaphore_signal(semaphore, inc=1, device_id=(other >> 1, other & 1), device_id_type=MESH)

    ring = [(me + 2) & (PEERS - 1), (me - 2) & (PEERS - 1)]
    entrance = ring + digit_mates(1, 4) + digit_mates(4, 16) + digit_mates(16, PEERS)
    for other in entrance:
        greet(barrier, other)
    for load in loads[1:]:
        load.start()

    loads[0].wait()

    def pack_edges(group, carry):
        at = pl.ds(pl.multiple_of(group * 8, 8), 8)
        for pack in range(packs):
            low = high = None
            for part in range(EDGES):
                plane = pack * EDGES + part
                if plane >= NTR * LEV:
                    continue
                value = tracers[plane // LEV, plane % LEV, at, :]
                low_at = (part + EDGES // 2) % EDGES
                to_low = pltpu.roll(value, low_at * HALO, 1) if low_at else value
                to_high = pltpu.roll(value, (part + 1) * HALO, 1) if part + 1 < EDGES else value
                low = to_low if part == 0 else jnp.where(lane // HALO == low_at, to_low, low)
                high = to_high if part == 0 else jnp.where(lane // HALO == part, to_high, high)
            edge_low[group, pack] = low
            edge_high[group, pack] = high
        return carry

    def edge_copies(piece):
        part = pl.ds(piece * PIECE, PIECE)
        return [
            pltpu.make_async_remote_copy(
                src_ref=source.at[part], dst_ref=target.at[part],
                send_sem=edge_sems.at[side, 0, piece], recv_sem=edge_sems.at[side, 1, piece],
                device_id=(lax.rem(lon + distance, bands), lat), device_id_type=MESH,
            )
            for side, source, target, distance in ((0, edge_low, from_east, bands - 1), (1, edge_high, from_west, 1))
        ]

    pieces = groups // PIECE
    for piece in range(pieces):
        lax.fori_loop(piece * PIECE, piece * PIECE + PIECE, pack_edges, 0, unroll=True)
        if piece == 0:
            pl.semaphore_wait(barrier, len(entrance))
        for copy in edge_copies(piece):
            copy.start()
    for other in digit_mates(1, 4):
        greet(ready.at[0], other)

    loads[1].wait()
    column = index[...]
    owner = lax.broadcasted_iota(jnp.int32, column.shape, 0)
    member_of = (owner // 16 - lon // 8) & 3
    row = column >> 7
    turn_by = (member_of - row) & 3
    place[...] = turn_by * (lat_rows * LANES // 4) + (row >> 2) * LANES + (column & (LANES - 1))
    to_scalars = pltpu.make_async_copy(place, address, address_sem)
    to_scalars.start()

    for load in loads[2:]:
        load.wait()

    def interior(group, carry):
        at = pl.ds(pl.multiple_of(group * 8, 8), 8)
        for level in range(LEV):
            cell = lane + offsets[level, at, :]
            weight = weights[level, at, :]
            west_weight = jnp.where((cell >= 0) & (cell < LANES), 1.0 - weight, 0.0)
            east_weight = jnp.where((cell >= -1) & (cell < LANES - 1), weight, 0.0)
            west_at = cell & (LANES - 1)
            east_at = (cell + 1) & (LANES - 1)
            for t in range(NTR):
                main = tracers[t, level, at, :]
                west = jnp.take_along_axis(main, west_at, axis=1)
                east = jnp.take_along_axis(main, east_at, axis=1)
                partial[t, level, at, :] = west_weight * west + east_weight * east
        inverses, uppers = factor_levels([diffusion[level, at, :] for level in range(LEV - 1)])
        for level in range(LEV):
            factors[level, at, :] = inverses[level]
        for level in range(LEV - 1):
            factors[LEV + level, at, :] = uppers[level]
        return carry

    lax.fori_loop(0, groups, interior, 0)
    pl.semaphore_wait(ready.at[0], 3)
    for other in digit_mates(4, 16):
        greet(ready.at[1], other)

    def finish(group, carry):
        at = pl.ds(pl.multiple_of(group * 8, 8), 8)
        values = [[None] * LEV for _ in range(NTR)]
        for level in range(LEV):
            cell = lane + offsets[level, at, :]
            weight = weights[level, at, :]
            west_weight = jnp.where((cell >= 0) & (cell < LANES), 0.0, 1.0 - weight)
            east_weight = jnp.where((cell >= -1) & (cell < LANES - 1), 0.0, weight)
            west_at = (cell & (HALO - 1)) + jnp.where(cell < 0, 0, LANES // 2)
            east_at = ((cell + 1) & (HALO - 1)) + jnp.where(cell < -1, 0, LANES // 2)
            for t in range(NTR):
                plane = t * LEV + level
                pack, part = plane // EDGES, plane % EDGES
                edge = jnp.where(lane // HALO == part, from_west[group, pack], from_east[group, pack])
                west = jnp.take_along_axis(edge, (west_at + part * HALO) & (LANES - 1), axis=1)
                east = jnp.take_along_axis(edge, (east_at + part * HALO) & (LANES - 1), axis=1)
                values[t][level] = partial[t, level, at, :] + (west_weight * west + east_weight * east)
        coefs = [diffusion[level, at, :] for level in range(LEV - 1)]
        inverses = [factors[level, at, :] for level in range(LEV)]
        uppers = [factors[LEV + level, at, :] for level in range(LEV - 1)]
        for t in range(NTR):
            solved = solve_levels(values[t], coefs, inverses, uppers)
            for level in range(LEV):
                rows[pl.ds(group * 8 * FEAT + level * NTR + t, 8, stride=FEAT), :] = solved[level]
        for spare in range(NTR * LEV, FEAT):
            rows[pl.ds(group * 8 * FEAT + spare, 8, stride=FEAT), :] = jnp.zeros((8, LANES), jnp.float32)
        return carry

    def turn(block, carry):
        at = pl.ds(pl.multiple_of(block * LANES, LANES), LANES)
        turned = rows[at, :].T
        for by in range(FOUR):
            table[by, at, :] = pltpu.roll(turned, by * FEAT, 1) if by else turned
        return carry

    def finish_piece(piece, carry):
        for copy in edge_copies(piece):
            copy.wait_recv()
        lax.fori_loop(piece * PIECE, piece * PIECE + PIECE, finish, 0)
        blocks = PIECE * 8 // FOUR
        for block in range(blocks):
            turn(piece * blocks + block, 0)
        return carry

    lax.fori_loop(0, pieces, finish_piece, 0)

    table_rows = table.reshape(FOUR * lat_rows * LANES // FOUR, LANES)

    x, y, z, core = (lon >> 3) & 3, lat * 2 + (lon >> 5), (lon >> 1) & 3, lon & 1

    def targets_of(step):
        away = step & 15
        to_core = (core + (step >> 4)) & 1
        targets = []
        for member in range(FOUR):
            to_x = (x + member) & 3
            to_y = (y + (away & 3) + member) & 3
            to_z = (z + ((away >> 2) + away) + member) & 3
            to_lon = ((to_y & 1) << 5) + (to_x << 3) + (to_z << 1) + to_core
            to_lat = to_y >> 1
            targets.append((to_lon, to_lat, to_lon * 2 + to_lat))
        return targets

    def gather(step, half):
        owners = [owner for _, _, owner in targets_of(step)]
        for eight in range(LANES // 8):
            wide = None
            for member in range(FOUR):
                tile = None
                for sublane in range(8):
                    at = address[owners[member], eight * 8 + sublane]
                    row = jnp.broadcast_to(table_rows[pl.ds(at, 1), :], (8, LANES))
                    tile = row if tile is None else jnp.where(sublanes == sublane, row, tile)
                wide = tile if wide is None else jnp.where(lane // FEAT == member, tile, wide)
            stage[half, eight * 8 : eight * 8 + 8, :] = wide

    def send(step, half, first=0):
        turned = stage[half].T
        for member, (to_lon, to_lat, owner) in enumerate(targets_of(step)):
            box = step * FOUR + member
            outbox[box] = turned[member * FEAT : (member + 1) * FEAT, :]
            length = count[0, owner].astype(jnp.float32)
            outbox[box, SENT - 1 : SENT, :] = jnp.full((1, LANES), length, jnp.float32)
            slot = (owner - me) & (PEERS - 1)
            if member >= first:
                pltpu.make_async_remote_copy(
                    src_ref=outbox.at[box, 0:SENT], dst_ref=arrived.at[slot, 0:SENT],
                    send_sem=send_sem, recv_sem=recv_sem,
                    device_id=(to_lon, to_lat), device_id_type=MESH,
                ).start()

    to_scalars.wait()
    pl.semaphore_wait(ready.at[1], 3)
    steps = PEERS // FOUR
    gather(0, 0)
    send(0, 0, first=1)
    gather(1, 1)

    def two_steps(turn_at, carry):
        send(2 * turn_at + 1, 1)
        gather(2 * turn_at + 2, 0)
        send(2 * turn_at + 2, 0)
        gather(2 * turn_at + 3, 1)
        return carry

    lax.fori_loop(0, steps // 2 - 1, two_steps, 0)
    send(steps - 1, 1)
    arrived[0] = outbox[0]
    others = pltpu.make_async_copy(outbox.at[1:PEERS, 0:SENT], arrived.at[1:PEERS, 0:SENT], recv_sem)
    others.wait()
    pltpu.make_async_copy(outbox.at[1:PEERS, 0:SENT], arrived.at[1:PEERS, 0:SENT], send_sem).wait()
    lengths[...] = arrived[:, SENT - 1, :].T[0:1, :].astype(jnp.int32)
    for piece in range(pieces):
        for copy in edge_copies(piece):
            copy.wait_send()


def place_kernel(arrived, lengths, out, owned, rows, out_sems):
    columns = out.shape[2]
    lane = lax.broadcasted_iota(jnp.int32, (FEAT, LANES), 1)

    def place(source, start):
        block = start // LANES
        shift = lax.rem(start, LANES)
        rolled = pltpu.roll(arrived[source], shift, 1)
        first = pl.ds(pl.multiple_of(block * FEAT, FEAT), FEAT)
        second = pl.ds(pl.multiple_of(block * FEAT + FEAT, FEAT), FEAT)
        pltpu.store(owned.at[first, :], rolled, mask=lane >= shift)
        owned[second, :] = rolled
        return start + lengths[0, source]

    lax.fori_loop(0, arrived.shape[0], place, jnp.int32(0), unroll=16)

    copies = []
    width = columns // OUT_PIECES
    for piece in range(OUT_PIECES):
        for block in range(piece * width // LANES, (piece + 1) * width // LANES):
            for level in range(LEV):
                begin = block * FEAT + level * NTR
                rows[level, :, block * LANES : (block + 1) * LANES] = owned[begin : begin + NTR, :]
        part = pl.ds(piece * width, width)
        copies.append(pltpu.make_async_copy(rows.at[:, :, part], out.at[:, :, part], out_sems.at[piece]))
        copies[-1].start()
    for copy in copies:
        copy.wait()


def body(tracers, offsets, weights, diffusion, send_index, send_count):
    lat_rows, lon_width = tracers.shape[2:]
    columns = lat_rows * lon_width
    groups = lat_rows // 8
    packs = -(-NTR * LEV // EDGES)
    vmem = pl.BlockSpec(memory_space=pltpu.VMEM)
    smem = pl.BlockSpec(memory_space=pltpu.SMEM)
    edge = pltpu.VMEM((groups, packs, 8, LANES), jnp.float32)
    arrived, lengths = pl.pallas_call(
        exchange_kernel,
        out_shape=(
            jax.ShapeDtypeStruct((PEERS, FEAT, LANES), jnp.float32),
            jax.ShapeDtypeStruct((1, PEERS), jnp.int32),
        ),
        in_specs=[pl.BlockSpec(memory_space=pltpu.HBM)] * 6,
        out_specs=(vmem, vmem),
        scratch_shapes=[
            pltpu.VMEM(tracers.shape, jnp.float32),
            pltpu.VMEM(offsets.shape, jnp.int32),
            pltpu.VMEM(weights.shape, jnp.float32),
            pltpu.VMEM(diffusion.shape, jnp.float32),
            pltpu.VMEM((PEERS, LANES), jnp.int32),
            pltpu.SMEM((1, PEERS), jnp.int32),
            pltpu.VMEM(tracers.shape, jnp.float32),
            pltpu.VMEM((2 * LEV - 1, lat_rows, lon_width), jnp.float32),
            edge, edge, edge, edge,
            pltpu.VMEM((lat_rows * FEAT, LANES), jnp.float32),
            pltpu.VMEM((FOUR, columns // FOUR, LANES), jnp.float32),
            pltpu.VMEM((2, LANES, LANES), jnp.float32),
            pltpu.VMEM((PEERS, FEAT, LANES), jnp.float32),
            pltpu.VMEM((PEERS, LANES), jnp.int32),
            pltpu.SMEM((PEERS, LANES), jnp.int32),
            pltpu.SemaphoreType.DMA((6,)),
            pltpu.SemaphoreType.DMA((2, 2, groups // PIECE)),
            pltpu.SemaphoreType.DMA,
            pltpu.SemaphoreType.DMA,
            pltpu.SemaphoreType.DMA,
            pltpu.SemaphoreType.REGULAR((2,)),
        ],
        compiler_params=pltpu.CompilerParams(vmem_limit_bytes=40 << 20, collective_id=0, has_side_effects=True),
        name="advect_solve_exchange",
    )(*(pltpu.with_memory_space_constraint(x, pltpu.HBM) for x in (tracers, offsets, weights, diffusion, send_index[0], send_count)))
    owned = pl.pallas_call(
        place_kernel,
        out_shape=jax.ShapeDtypeStruct((LEV, NTR, columns), jnp.float32),
        in_specs=[vmem, smem],
        out_specs=pl.BlockSpec(memory_space=pltpu.HBM),
        scratch_shapes=[
            pltpu.VMEM(((columns // LANES + 2) * FEAT, LANES), jnp.float32),
            pltpu.VMEM((LEV, NTR, columns), jnp.float32),
            pltpu.SemaphoreType.DMA((OUT_PIECES,)),
        ],
        compiler_params=pltpu.CompilerParams(vmem_limit_bytes=32 << 20),
        name="place_owned",
    )(arrived, lengths)
    return jnp.transpose(owned, (1, 0, 2))


def solution(mesh):
    return jax.shard_map(
        body,
        mesh=mesh,
        in_specs=(
            P(None, None, "lat", "lon"),
            P(None, "lat", "lon"),
            P(None, "lat", "lon"),
            P(None, "lat", "lon"),
            P(("lon", "lat"), None, None),
            P(("lon", "lat"), None),
        ),
        out_specs=P(None, None, ("lon", "lat")),
        check_vma=False,
    )
```

```python
import jax
import jax.numpy as jnp
from jax import lax
from jax.experimental import pallas as pl
from jax.experimental.pallas import tpu as pltpu
from jax.sharding import PartitionSpec as P

NTR = 3
LEV = 10
HALO = 16
FEAT = 32
SENT = NTR * LEV
FAR_OUT = 1000.0
LANES = 128
FOUR = LANES // FEAT
EDGES = LANES // HALO
PEERS = 128
PIECE = 2
OUT_PIECES = 4
AXES = ("lon", "lat")
MESH = pl.DeviceIdType.MESH


def factor_levels(coefs):
    inverses, uppers = [], []
    for level in range(LEV):
        denom = jnp.ones_like(coefs[0])
        if level > 0:
            denom = denom + coefs[level - 1]
        if level < LEV - 1:
            denom = denom + coefs[level]
        if level > 0:
            denom = denom - coefs[level - 1] * uppers[level - 1]
        inverses.append(1.0 / denom)
        if level < LEV - 1:
            uppers.append(coefs[level] * inverses[level])
    return inverses, uppers


def solve_levels(values, coefs, inverses, uppers):
    reduced = []
    for level in range(LEV):
        right = values[level]
        if level > 0:
            right = right + coefs[level - 1] * reduced[level - 1]
        reduced.append(right * inverses[level])
    output = [None] * LEV
    output[LEV - 1] = reduced[LEV - 1]
    for level in range(LEV - 2, -1, -1):
        output[level] = reduced[level] + uppers[level] * output[level + 1]
    return output


def exchange_kernel(
    tracers_hbm, offsets_hbm, weights_hbm, diffusion_hbm, index_hbm, count_hbm, arrived, lengths,
    tracers, offsets, weights, diffusion, index, count, partial, factors,
    edge_low, edge_high, from_east, from_west, rows, table, stage, outbox, place, address,
    load_sems, edge_sems, address_sem, send_sem, recv_sem, ready,
):
    pairs = (
        (tracers_hbm, tracers), (index_hbm, index), (offsets_hbm, offsets),
        (weights_hbm, weights), (diffusion_hbm, diffusion), (count_hbm, count),
    )
    loads = [pltpu.make_async_copy(source, here, load_sems.at[i]) for i, (source, here) in enumerate(pairs)]
    loads[0].start()
    lat_rows = tracers.shape[2]
    groups = lat_rows // 8
    packs = from_east.shape[1]
    lon, lat = lax.axis_index("lon"), lax.axis_index("lat")
    bands = lax.axis_size("lon")
    me = lon * 2 + lat
    lane = lax.broadcasted_iota(jnp.int32, (8, LANES), 1)
    sublanes = lax.broadcasted_iota(jnp.int32, (8, LANES), 0)

    barrier = pltpu.get_barrier_semaphore()

    def digit_mates(low, span):
        mask = span - low
        return [(me & (PEERS - 1 - mask)) + ((me + low * step) & mask) for step in range(1, span // low)]

    def greet(semaphore, other):
        pl.semaphore_signal(semaphore, inc=1, device_id=(other >> 1, other & 1), device_id_type=MESH)

    ring = [(me + 2) & (PEERS - 1), (me - 2) & (PEERS - 1)]
    entrance = ring + digit_mates(1, 4) + digit_mates(4, 16) + digit_mates(16, PEERS)
    for other in entrance:
        greet(barrier, other)
    for load in loads[1:]:
        load.start()

    loads[0].wait()

    def pack_edges(group, carry):
        at = pl.ds(pl.multiple_of(group * 8, 8), 8)
        for pack in range(packs):
            low = high = None
            for part in range(EDGES):
                plane = pack * EDGES + part
                if plane >= NTR * LEV:
                    continue
                value = tracers[plane // LEV, plane % LEV, at, :]
                low_at = (part + EDGES // 2) % EDGES
                to_low = pltpu.roll(value, low_at * HALO, 1) if low_at else value
                to_high = pltpu.roll(value, (part + 1) * HALO, 1) if part + 1 < EDGES else value
                low = to_low if part == 0 else jnp.where(lane // HALO == low_at, to_low, low)
                high = to_high if part == 0 else jnp.where(lane // HALO == part, to_high, high)
            edge_low[group, pack] = low
            edge_high[group, pack] = high
        return carry

    def edge_copies(piece):
        part = pl.ds(piece * PIECE, PIECE)
        return [
            pltpu.make_async_remote_copy(
                src_ref=source.at[part], dst_ref=target.at[part],
                send_sem=edge_sems.at[side, 0, piece], recv_sem=edge_sems.at[side, 1, piece],
                device_id=(lax.rem(lon + distance, bands), lat), device_id_type=MESH,
            )
            for side, source, target, distance in ((0, edge_low, from_east, bands - 1), (1, edge_high, from_west, 1))
        ]

    pieces = groups // PIECE
    for piece in range(pieces):
        lax.fori_loop(piece * PIECE, piece * PIECE + PIECE, pack_edges, 0, unroll=True)
        if piece == 0:
            pl.semaphore_wait(barrier, len(entrance))
        for copy in edge_copies(piece):
            copy.start()
    for other in digit_mates(1, 4):
        greet(ready.at[0], other)

    loads[1].wait()
    column = index[...]
    owner = lax.broadcasted_iota(jnp.int32, column.shape, 0)
    member_of = (owner // 16 - lon // 8) & 3
    row = column >> 7
    turn_by = (member_of - row) & 3
    place[...] = turn_by * (lat_rows * LANES // 4) + (row >> 2) * LANES + (column & (LANES - 1))
    to_scalars = pltpu.make_async_copy(place, address, address_sem)
    to_scalars.start()

    for load in loads[2:]:
        load.wait()

    def interior(group, carry):
        at = pl.ds(pl.multiple_of(group * 8, 8), 8)
        for level in range(LEV):
            cell = lane + offsets[level, at, :]
            weight = weights[level, at, :]
            west_weight = jnp.where((cell >= 0) & (cell < LANES), 1.0 - weight, 0.0)
            east_weight = jnp.where((cell >= -1) & (cell < LANES - 1), weight, 0.0)
            west_at = cell & (LANES - 1)
            east_at = (cell + 1) & (LANES - 1)
            for t in range(NTR):
                main = tracers[t, level, at, :]
                west = jnp.take_along_axis(main, west_at, axis=1)
                east = jnp.take_along_axis(main, east_at, axis=1)
                partial[t, level, at, :] = west_weight * west + east_weight * east
        inverses, uppers = factor_levels([diffusion[level, at, :] for level in range(LEV - 1)])
        for level in range(LEV):
            factors[level, at, :] = inverses[level]
        for level in range(LEV - 1):
            factors[LEV + level, at, :] = uppers[level]
        return carry

    lax.fori_loop(0, groups, interior, 0)
    pl.semaphore_wait(ready.at[0], 3)
    for other in digit_mates(4, 16):
        greet(ready.at[1], other)

    def finish(group, carry):
        at = pl.ds(pl.multiple_of(group * 8, 8), 8)
        values = [[None] * LEV for _ in range(NTR)]
        for level in range(LEV):
            cell = lane + offsets[level, at, :]
            weight = weights[level, at, :]
            west_weight = jnp.where((cell >= 0) & (cell < LANES), 0.0, 1.0 - weight)
            east_weight = jnp.where((cell >= -1) & (cell < LANES - 1), 0.0, weight)
            west_at = (cell & (HALO - 1)) + jnp.where(cell < 0, 0, LANES // 2)
            east_at = ((cell + 1) & (HALO - 1)) + jnp.where(cell < -1, 0, LANES // 2)
            for t in range(NTR):
                plane = t * LEV + level
                pack, part = plane // EDGES, plane % EDGES
                edge = jnp.where(lane // HALO == part, from_west[group, pack], from_east[group, pack])
                west = jnp.take_along_axis(edge, (west_at + part * HALO) & (LANES - 1), axis=1)
                east = jnp.take_along_axis(edge, (east_at + part * HALO) & (LANES - 1), axis=1)
                values[t][level] = partial[t, level, at, :] + (west_weight * west + east_weight * east)
        coefs = [diffusion[level, at, :] for level in range(LEV - 1)]
        inverses = [factors[level, at, :] for level in range(LEV)]
        uppers = [factors[LEV + level, at, :] for level in range(LEV - 1)]
        for t in range(NTR):
            solved = solve_levels(values[t], coefs, inverses, uppers)
            for level in range(LEV):
                rows[pl.ds(group * 8 * FEAT + level * NTR + t, 8, stride=FEAT), :] = solved[level]
        for spare in range(NTR * LEV, FEAT):
            rows[pl.ds(group * 8 * FEAT + spare, 8, stride=FEAT), :] = jnp.zeros((8, LANES), jnp.float32)
        return carry

    def turn(block, carry):
        at = pl.ds(pl.multiple_of(block * LANES, LANES), LANES)
        turned = rows[at, :].T
        for by in range(FOUR):
            table[by, at, :] = pltpu.roll(turned, by * FEAT, 1) if by else turned
        return carry

    def finish_piece(piece, carry):
        for copy in edge_copies(piece):
            copy.wait_recv()
        lax.fori_loop(piece * PIECE, piece * PIECE + PIECE, finish, 0)
        blocks = PIECE * 8 // FOUR
        for block in range(blocks):
            turn(piece * blocks + block, 0)
        return carry

    lax.fori_loop(0, pieces, finish_piece, 0)

    table_rows = table.reshape(FOUR * lat_rows * LANES // FOUR, LANES)

    x, y, z, core = (lon >> 3) & 3, lat * 2 + (lon >> 5), (lon >> 1) & 3, lon & 1

    def targets_of(step):
        away = step & 15
        to_core = (core + (step >> 4)) & 1
        targets = []
        for member in range(FOUR):
            to_x = (x + member) & 3
            to_y = (y + (away & 3) + member) & 3
            to_z = (z + ((away >> 2) + away) + member) & 3
            to_lon = ((to_y & 1) << 5) + (to_x << 3) + (to_z << 1) + to_core
            to_lat = to_y >> 1
            targets.append((to_lon, to_lat, to_lon * 2 + to_lat))
        return targets

    def gather(step, half):
        owners = [owner for _, _, owner in targets_of(step)]
        for eight in range(LANES // 8):
            wide = None
            for member in range(FOUR):
                tile = None
                for sublane in range(8):
                    at = address[owners[member], eight * 8 + sublane]
                    row = jnp.broadcast_to(table_rows[pl.ds(at, 1), :], (8, LANES))
                    tile = row if tile is None else jnp.where(sublanes == sublane, row, tile)
                wide = tile if wide is None else jnp.where(lane // FEAT == member, tile, wide)
            stage[half, eight * 8 : eight * 8 + 8, :] = wide

    def send(step, half):
        turned = stage[half].T
        for member, (to_lon, to_lat, owner) in enumerate(targets_of(step)):
            box = step * FOUR + member
            outbox[box] = turned[member * FEAT : (member + 1) * FEAT, :]
            length = jnp.full((1, LANES), count[0, owner].astype(jnp.float32), jnp.float32)
            unused = (lane[0:1] == LANES - 1) & (length < LANES)
            outbox[box, 0:1, :] = jnp.where(unused, length + FAR_OUT, turned[member * FEAT : member * FEAT + 1, :])
            slot = (owner - me) & (PEERS - 1)

            def start():
                pltpu.make_async_remote_copy(
                    src_ref=outbox.at[box, 0:SENT], dst_ref=arrived.at[slot, 0:SENT],
                    send_sem=send_sem, recv_sem=recv_sem,
                    device_id=(to_lon, to_lat), device_id_type=MESH,
                ).start()

            if member or half:
                start()
            else:
                pl.when(step > 0)(start)

    to_scalars.wait()
    pl.semaphore_wait(ready.at[1], 3)
    steps = PEERS // FOUR
    def two_steps(turn_at, carry):
        for half in range(2):
            gather(2 * turn_at + half, half)
            send(2 * turn_at + half, half)
        return carry

    lax.fori_loop(0, steps // 2, two_steps, 0)
    arrived[0] = outbox[0]
    others = pltpu.make_async_copy(outbox.at[1:PEERS, 0:SENT], arrived.at[1:PEERS, 0:SENT], recv_sem)
    others.wait()
    pltpu.make_async_copy(outbox.at[1:PEERS, 0:SENT], arrived.at[1:PEERS, 0:SENT], send_sem).wait()
    last = arrived[:, 0, :].T[LANES - 1 : LANES, :]
    lengths[...] = jnp.where(last > FAR_OUT / 2, last - FAR_OUT, LANES).astype(jnp.int32)
    for piece in range(pieces):
        for copy in edge_copies(piece):
            copy.wait_send()


def place_kernel(arrived, lengths, out, owned, rows, out_sems):
    columns = out.shape[2]
    lane = lax.broadcasted_iota(jnp.int32, (FEAT, LANES), 1)

    def place(source, start):
        block = start // LANES
        shift = lax.rem(start, LANES)
        rolled = pltpu.roll(arrived[source], shift, 1)
        first = pl.ds(pl.multiple_of(block * FEAT, FEAT), FEAT)
        second = pl.ds(pl.multiple_of(block * FEAT + FEAT, FEAT), FEAT)
        pltpu.store(owned.at[first, :], rolled, mask=lane >= shift)
        owned[second, :] = rolled
        return start + lengths[0, source]

    lax.fori_loop(0, arrived.shape[0], place, jnp.int32(0), unroll=16)

    copies = []
    width = columns // OUT_PIECES
    for piece in range(OUT_PIECES):
        for block in range(piece * width // LANES, (piece + 1) * width // LANES):
            for level in range(LEV):
                begin = block * FEAT + level * NTR
                rows[level, :, block * LANES : (block + 1) * LANES] = owned[begin : begin + NTR, :]
        part = pl.ds(piece * width, width)
        copies.append(pltpu.make_async_copy(rows.at[:, :, part], out.at[:, :, part], out_sems.at[piece]))
        copies[-1].start()
    for copy in copies:
        copy.wait()


def body(tracers, offsets, weights, diffusion, send_index, send_count):
    lat_rows, lon_width = tracers.shape[2:]
    columns = lat_rows * lon_width
    groups = lat_rows // 8
    packs = -(-NTR * LEV // EDGES)
    vmem = pl.BlockSpec(memory_space=pltpu.VMEM)
    smem = pl.BlockSpec(memory_space=pltpu.SMEM)
    edge = pltpu.VMEM((groups, packs, 8, LANES), jnp.float32)
    arrived, lengths = pl.pallas_call(
        exchange_kernel,
        out_shape=(
            jax.ShapeDtypeStruct((PEERS, FEAT, LANES), jnp.float32),
            jax.ShapeDtypeStruct((1, PEERS), jnp.int32),
        ),
        in_specs=[pl.BlockSpec(memory_space=pltpu.HBM)] * 6,
        out_specs=(vmem, vmem),
        scratch_shapes=[
            pltpu.VMEM(tracers.shape, jnp.float32),
            pltpu.VMEM(offsets.shape, jnp.int32),
            pltpu.VMEM(weights.shape, jnp.float32),
            pltpu.VMEM(diffusion.shape, jnp.float32),
            pltpu.VMEM((PEERS, LANES), jnp.int32),
            pltpu.SMEM((1, PEERS), jnp.int32),
            pltpu.VMEM(tracers.shape, jnp.float32),
            pltpu.VMEM((2 * LEV - 1, lat_rows, lon_width), jnp.float32),
            edge, edge, edge, edge,
            pltpu.VMEM((lat_rows * FEAT, LANES), jnp.float32),
            pltpu.VMEM((FOUR, columns // FOUR, LANES), jnp.float32),
            pltpu.VMEM((2, LANES, LANES), jnp.float32),
            pltpu.VMEM((PEERS, FEAT, LANES), jnp.float32),
            pltpu.VMEM((PEERS, LANES), jnp.int32),
            pltpu.SMEM((PEERS, LANES), jnp.int32),
            pltpu.SemaphoreType.DMA((6,)),
            pltpu.SemaphoreType.DMA((2, 2, groups // PIECE)),
            pltpu.SemaphoreType.DMA,
            pltpu.SemaphoreType.DMA,
            pltpu.SemaphoreType.DMA,
            pltpu.SemaphoreType.REGULAR((2,)),
        ],
        compiler_params=pltpu.CompilerParams(vmem_limit_bytes=40 << 20, collective_id=0, has_side_effects=True),
        name="advect_solve_exchange",
    )(*(pltpu.with_memory_space_constraint(x, pltpu.HBM) for x in (tracers, offsets, weights, diffusion, send_index[0], send_count)))
    owned = pl.pallas_call(
        place_kernel,
        out_shape=jax.ShapeDtypeStruct((LEV, NTR, columns), jnp.float32),
        in_specs=[vmem, smem],
        out_specs=pl.BlockSpec(memory_space=pltpu.HBM),
        scratch_shapes=[
            pltpu.VMEM(((columns // LANES + 2) * FEAT, LANES), jnp.float32),
            pltpu.VMEM((LEV, NTR, columns), jnp.float32),
            pltpu.SemaphoreType.DMA((OUT_PIECES,)),
        ],
        compiler_params=pltpu.CompilerParams(vmem_limit_bytes=32 << 20),
        name="place_owned",
    )(arrived, lengths)
    return jnp.transpose(owned, (1, 0, 2))


def solution(mesh):
    return jax.shard_map(
        body,
        mesh=mesh,
        in_specs=(
            P(None, None, "lat", "lon"),
            P(None, "lat", "lon"),
            P(None, "lat", "lon"),
            P(None, "lat", "lon"),
            P(("lon", "lat"), None, None),
            P(("lon", "lat"), None),
        ),
        out_specs=P(None, None, ("lon", "lat")),
        check_vma=False,
    )
```

```python
import jax
import jax.numpy as jnp
from jax import lax
from jax.experimental import pallas as pl
from jax.experimental.pallas import tpu as pltpu
from jax.sharding import PartitionSpec as P

NTR = 3
LEV = 10
HALO = 16
FEAT = 32
SENT = NTR * LEV
FAR_OUT = 1000.0
LANES = 128
FOUR = LANES // FEAT
EDGES = LANES // HALO
PEERS = 128
PIECE = 2
OUT_PIECES = 2
AXES = ("lon", "lat")
MESH = pl.DeviceIdType.MESH


def factor_levels(coefs):
    inverses, uppers = [], []
    for level in range(LEV):
        denom = jnp.ones_like(coefs[0])
        if level > 0:
            denom = denom + coefs[level - 1]
        if level < LEV - 1:
            denom = denom + coefs[level]
        if level > 0:
            denom = denom - coefs[level - 1] * uppers[level - 1]
        inverses.append(1.0 / denom)
        if level < LEV - 1:
            uppers.append(coefs[level] * inverses[level])
    return inverses, uppers


def solve_levels(values, coefs, inverses, uppers):
    reduced = []
    for level in range(LEV):
        right = values[level]
        if level > 0:
            right = right + coefs[level - 1] * reduced[level - 1]
        reduced.append(right * inverses[level])
    output = [None] * LEV
    output[LEV - 1] = reduced[LEV - 1]
    for level in range(LEV - 2, -1, -1):
        output[level] = reduced[level] + uppers[level] * output[level + 1]
    return output


def exchange_kernel(
    tracers_hbm, offsets_hbm, weights_hbm, diffusion_hbm, index_hbm, count_hbm, arrived, lengths,
    tracers, offsets, weights, diffusion, index, count, partial, factors,
    edge_low, edge_high, from_east, from_west, rows, table, stage, outbox, place, address,
    load_sems, edge_sems, address_sem, send_sem, recv_sem, ready,
):
    pairs = (
        (tracers_hbm, tracers), (index_hbm, index), (offsets_hbm, offsets),
        (weights_hbm, weights), (diffusion_hbm, diffusion), (count_hbm, count),
    )
    loads = [pltpu.make_async_copy(source, here, load_sems.at[i]) for i, (source, here) in enumerate(pairs)]
    loads[0].start()
    lat_rows = tracers.shape[2]
    groups = lat_rows // 8
    packs = from_east.shape[1]
    lon, lat = lax.axis_index("lon"), lax.axis_index("lat")
    bands = lax.axis_size("lon")
    me = lon * 2 + lat
    lane = lax.broadcasted_iota(jnp.int32, (8, LANES), 1)
    sublanes = lax.broadcasted_iota(jnp.int32, (8, LANES), 0)

    barrier = pltpu.get_barrier_semaphore()

    def digit_mates(low, span):
        mask = span - low
        return [(me & (PEERS - 1 - mask)) + ((me + low * step) & mask) for step in range(1, span // low)]

    def greet(semaphore, other):
        pl.semaphore_signal(semaphore, inc=1, device_id=(other >> 1, other & 1), device_id_type=MESH)

    ring = [(me + 2) & (PEERS - 1), (me - 2) & (PEERS - 1)]
    entrance = ring + digit_mates(1, 4) + digit_mates(4, 16) + digit_mates(16, PEERS)
    for other in entrance:
        greet(barrier, other)
    for load in loads[1:]:
        load.start()

    loads[0].wait()

    def pack_edges(group, carry):
        at = pl.ds(pl.multiple_of(group * 8, 8), 8)
        for pack in range(packs):
            low = high = None
            for part in range(EDGES):
                plane = pack * EDGES + part
                if plane >= NTR * LEV:
                    continue
                value = tracers[plane // LEV, plane % LEV, at, :]
                low_at = (part + EDGES // 2) % EDGES
                to_low = pltpu.roll(value, low_at * HALO, 1) if low_at else value
                to_high = pltpu.roll(value, (part + 1) * HALO, 1) if part + 1 < EDGES else value
                low = to_low if part == 0 else jnp.where(lane // HALO == low_at, to_low, low)
                high = to_high if part == 0 else jnp.where(lane // HALO == part, to_high, high)
            edge_low[group, pack] = low
            edge_high[group, pack] = high
        return carry

    def edge_copies(piece):
        part = pl.ds(piece * PIECE, PIECE)
        return [
            pltpu.make_async_remote_copy(
                src_ref=source.at[part], dst_ref=target.at[part],
                send_sem=edge_sems.at[side, 0, piece], recv_sem=edge_sems.at[side, 1, piece],
                device_id=(lax.rem(lon + distance, bands), lat), device_id_type=MESH,
            )
            for side, source, target, distance in ((0, edge_low, from_east, bands - 1), (1, edge_high, from_west, 1))
        ]

    pieces = groups // PIECE
    for piece in range(pieces):
        lax.fori_loop(piece * PIECE, piece * PIECE + PIECE, pack_edges, 0, unroll=True)
        if piece == 0:
            pl.semaphore_wait(barrier, len(entrance))
        for copy in edge_copies(piece):
            copy.start()
    for other in digit_mates(1, 4):
        greet(ready.at[0], other)

    loads[1].wait()
    column = index[...]
    owner = lax.broadcasted_iota(jnp.int32, column.shape, 0)
    member_of = (owner // 16 - lon // 8) & 3
    row = column >> 7
    turn_by = (member_of - row) & 3
    place[...] = turn_by * (lat_rows * LANES // 4) + (row >> 2) * LANES + (column & (LANES - 1))
    to_scalars = pltpu.make_async_copy(place, address, address_sem)
    to_scalars.start()

    for load in loads[2:]:
        load.wait()

    def interior(group, carry):
        at = pl.ds(pl.multiple_of(group * 8, 8), 8)
        for level in range(LEV):
            cell = lane + offsets[level, at, :]
            weight = weights[level, at, :]
            west_weight = jnp.where((cell >= 0) & (cell < LANES), 1.0 - weight, 0.0)
            east_weight = jnp.where((cell >= -1) & (cell < LANES - 1), weight, 0.0)
            west_at = cell & (LANES - 1)
            east_at = (cell + 1) & (LANES - 1)
            for t in range(NTR):
                main = tracers[t, level, at, :]
                west = jnp.take_along_axis(main, west_at, axis=1)
                east = jnp.take_along_axis(main, east_at, axis=1)
                partial[t, level, at, :] = west_weight * west + east_weight * east
        inverses, uppers = factor_levels([diffusion[level, at, :] for level in range(LEV - 1)])
        for level in range(LEV):
            factors[level, at, :] = inverses[level]
        for level in range(LEV - 1):
            factors[LEV + level, at, :] = uppers[level]
        return carry

    lax.fori_loop(0, groups, interior, 0, unroll=8)
    pl.semaphore_wait(ready.at[0], 3)
    for other in digit_mates(4, 16):
        greet(ready.at[1], other)

    def finish(group):
        at = pl.ds(group * 8, 8)
        values = [[None] * LEV for _ in range(NTR)]
        for level in range(LEV):
            cell = lane + offsets[level, at, :]
            weight = weights[level, at, :]
            west_weight = jnp.where((cell >= 0) & (cell < LANES), 0.0, 1.0 - weight)
            east_weight = jnp.where((cell >= -1) & (cell < LANES - 1), 0.0, weight)
            west_at = (cell & (HALO - 1)) + jnp.where(cell < 0, 0, LANES // 2)
            east_at = ((cell + 1) & (HALO - 1)) + jnp.where(cell < -1, 0, LANES // 2)
            for t in range(NTR):
                plane = t * LEV + level
                pack, part = plane // EDGES, plane % EDGES
                edge = jnp.where(lane // HALO == part, from_west[group, pack], from_east[group, pack])
                west = jnp.take_along_axis(edge, (west_at + part * HALO) & (LANES - 1), axis=1)
                east = jnp.take_along_axis(edge, (east_at + part * HALO) & (LANES - 1), axis=1)
                values[t][level] = partial[t, level, at, :] + (west_weight * west + east_weight * east)
        coefs = [diffusion[level, at, :] for level in range(LEV - 1)]
        inverses = [factors[level, at, :] for level in range(LEV)]
        uppers = [factors[LEV + level, at, :] for level in range(LEV - 1)]
        for t in range(NTR):
            solved = solve_levels(values[t], coefs, inverses, uppers)
            for level in range(LEV):
                rows[pl.ds(group * 8 * FEAT + level * NTR + t, 8, stride=FEAT), :] = solved[level]
        for spare in range(NTR * LEV, FEAT):
            rows[pl.ds(group * 8 * FEAT + spare, 8, stride=FEAT), :] = jnp.zeros((8, LANES), jnp.float32)

    def turn(block):
        at = pl.ds(block * LANES, LANES)
        turned = rows[at, :].T
        for by in range(FOUR):
            table[by, at, :] = pltpu.roll(turned, by * FEAT, 1) if by else turned

    blocks = PIECE * 8 // FOUR
    for piece in range(pieces + 1):
        if piece < pieces:
            for copy in edge_copies(piece):
                copy.wait_recv()
        for part in range(PIECE):
            if piece < pieces:
                finish(piece * PIECE + part)
            if piece:
                for block in range(blocks // PIECE):
                    turn((piece - 1) * blocks + part * (blocks // PIECE) + block)

    table_rows = table.reshape(FOUR * lat_rows * LANES // FOUR, LANES)

    x, y, z, core = (lon >> 3) & 3, lat * 2 + (lon >> 5), (lon >> 1) & 3, lon & 1

    def targets_of(step):
        away = step & 15
        to_core = (core + (step >> 4)) & 1
        targets = []
        for member in range(FOUR):
            to_x = (x + member) & 3
            to_y = (y + (away & 3) + member) & 3
            to_z = (z + ((away >> 2) + away) + member) & 3
            to_lon = ((to_y & 1) << 5) + (to_x << 3) + (to_z << 1) + to_core
            to_lat = to_y >> 1
            targets.append((to_lon, to_lat, to_lon * 2 + to_lat))
        return targets

    def gather(step, half):
        owners = [owner for _, _, owner in targets_of(step)]
        for eight in range(LANES // 8):
            wide = None
            for member in range(FOUR):
                tile = None
                for sublane in range(8):
                    at = address[owners[member], eight * 8 + sublane]
                    row = jnp.broadcast_to(table_rows[pl.ds(at, 1), :], (8, LANES))
                    tile = row if tile is None else jnp.where(sublanes == sublane, row, tile)
                wide = tile if wide is None else jnp.where(lane // FEAT == member, tile, wide)
            stage[half, eight * 8 : eight * 8 + 8, :] = wide

    def send(step, half):
        turned = stage[half].T
        for member, (to_lon, to_lat, owner) in enumerate(targets_of(step)):
            box = step * FOUR + member
            outbox[box] = turned[member * FEAT : (member + 1) * FEAT, :]
            length = jnp.full((1, LANES), count[0, owner].astype(jnp.float32), jnp.float32)
            unused = (lane[0:1] == LANES - 1) & (length < LANES)
            outbox[box, 0:1, :] = jnp.where(unused, length + FAR_OUT, turned[member * FEAT : member * FEAT + 1, :])
            slot = (owner - me) & (PEERS - 1)

            def start():
                pltpu.make_async_remote_copy(
                    src_ref=outbox.at[box, 0:SENT], dst_ref=arrived.at[slot, 0:SENT],
                    send_sem=send_sem, recv_sem=recv_sem,
                    device_id=(to_lon, to_lat), device_id_type=MESH,
                ).start()

            if member or half:
                start()
            else:
                pl.when(step > 0)(start)

    to_scalars.wait()
    pl.semaphore_wait(ready.at[1], 3)
    steps = PEERS // FOUR
    def two_steps(turn_at, carry):
        for half in range(2):
            gather(2 * turn_at + half, half)
            send(2 * turn_at + half, half)
        return carry

    lax.fori_loop(0, steps // 2, two_steps, 0)
    arrived[0] = outbox[0]
    others = pltpu.make_async_copy(outbox.at[1:PEERS, 0:SENT], arrived.at[1:PEERS, 0:SENT], recv_sem)
    others.wait()
    pltpu.make_async_copy(outbox.at[1:PEERS, 0:SENT], arrived.at[1:PEERS, 0:SENT], send_sem).wait()
    last = arrived[:, 0, :].T[LANES - 1 : LANES, :]
    lengths[...] = jnp.where(last > FAR_OUT / 2, last - FAR_OUT, LANES).astype(jnp.int32)
    for piece in range(pieces):
        for copy in edge_copies(piece):
            copy.wait_send()


def place_kernel(arrived, lengths, out, owned, rows, out_sems):
    columns = out.shape[2]
    lane = lax.broadcasted_iota(jnp.int32, (FEAT, LANES), 1)

    def place(source, start):
        block = start // LANES
        shift = lax.rem(start, LANES)
        rolled = pltpu.roll(arrived[source], shift, 1)
        first = pl.ds(pl.multiple_of(block * FEAT, FEAT), FEAT)
        second = pl.ds(pl.multiple_of(block * FEAT + FEAT, FEAT), FEAT)
        pltpu.store(owned.at[first, :], rolled, mask=lane >= shift)
        owned[second, :] = rolled
        return start + lengths[0, source]

    lax.fori_loop(0, arrived.shape[0], place, jnp.int32(0), unroll=32)

    copies = []
    width = columns // OUT_PIECES
    for piece in range(OUT_PIECES):
        for block in range(piece * width // LANES, (piece + 1) * width // LANES):
            for level in range(LEV):
                begin = block * FEAT + level * NTR
                rows[level, :, block * LANES : (block + 1) * LANES] = owned[begin : begin + NTR, :]
        part = pl.ds(piece * width, width)
        copies.append(pltpu.make_async_copy(rows.at[:, :, part], out.at[:, :, part], out_sems.at[piece]))
        copies[-1].start()
    for copy in copies:
        copy.wait()


def body(tracers, offsets, weights, diffusion, send_index, send_count):
    lat_rows, lon_width = tracers.shape[2:]
    columns = lat_rows * lon_width
    groups = lat_rows // 8
    packs = -(-NTR * LEV // EDGES)
    vmem = pl.BlockSpec(memory_space=pltpu.VMEM)
    smem = pl.BlockSpec(memory_space=pltpu.SMEM)
    edge = pltpu.VMEM((groups, packs, 8, LANES), jnp.float32)
    arrived, lengths = pl.pallas_call(
        exchange_kernel,
        out_shape=(
            jax.ShapeDtypeStruct((PEERS, FEAT, LANES), jnp.float32),
            jax.ShapeDtypeStruct((1, PEERS), jnp.int32),
        ),
        in_specs=[pl.BlockSpec(memory_space=pltpu.HBM)] * 6,
        out_specs=(vmem, vmem),
        scratch_shapes=[
            pltpu.VMEM(tracers.shape, jnp.float32),
            pltpu.VMEM(offsets.shape, jnp.int32),
            pltpu.VMEM(weights.shape, jnp.float32),
            pltpu.VMEM(diffusion.shape, jnp.float32),
            pltpu.VMEM((PEERS, LANES), jnp.int32),
            pltpu.SMEM((1, PEERS), jnp.int32),
            pltpu.VMEM(tracers.shape, jnp.float32),
            pltpu.VMEM((2 * LEV - 1, lat_rows, lon_width), jnp.float32),
            edge, edge, edge, edge,
            pltpu.VMEM((lat_rows * FEAT, LANES), jnp.float32),
            pltpu.VMEM((FOUR, columns // FOUR, LANES), jnp.float32),
            pltpu.VMEM((2, LANES, LANES), jnp.float32),
            pltpu.VMEM((PEERS, FEAT, LANES), jnp.float32),
            pltpu.VMEM((PEERS, LANES), jnp.int32),
            pltpu.SMEM((PEERS, LANES), jnp.int32),
            pltpu.SemaphoreType.DMA((6,)),
            pltpu.SemaphoreType.DMA((2, 2, groups // PIECE)),
            pltpu.SemaphoreType.DMA,
            pltpu.SemaphoreType.DMA,
            pltpu.SemaphoreType.DMA,
            pltpu.SemaphoreType.REGULAR((2,)),
        ],
        compiler_params=pltpu.CompilerParams(vmem_limit_bytes=40 << 20, collective_id=0, has_side_effects=True),
        name="advect_solve_exchange",
    )(*(pltpu.with_memory_space_constraint(x, pltpu.HBM) for x in (tracers, offsets, weights, diffusion, send_index[0], send_count)))
    owned = pl.pallas_call(
        place_kernel,
        out_shape=jax.ShapeDtypeStruct((LEV, NTR, columns), jnp.float32),
        in_specs=[vmem, smem],
        out_specs=pl.BlockSpec(memory_space=pltpu.HBM),
        scratch_shapes=[
            pltpu.VMEM(((columns // LANES + 2) * FEAT, LANES), jnp.float32),
            pltpu.VMEM((LEV, NTR, columns), jnp.float32),
            pltpu.SemaphoreType.DMA((OUT_PIECES,)),
        ],
        compiler_params=pltpu.CompilerParams(vmem_limit_bytes=32 << 20),
        name="place_owned",
    )(arrived, lengths)
    return jnp.transpose(owned, (1, 0, 2))


def solution(mesh):
    return jax.shard_map(
        body,
        mesh=mesh,
        in_specs=(
            P(None, None, "lat", "lon"),
            P(None, "lat", "lon"),
            P(None, "lat", "lon"),
            P(None, "lat", "lon"),
            P(("lon", "lat"), None, None),
            P(("lon", "lat"), None),
        ),
        out_specs=P(None, None, ("lon", "lat")),
        check_vma=False,
    )
```

```python
import jax
import jax.numpy as jnp
from jax import lax
from jax.experimental import pallas as pl
from jax.experimental.pallas import tpu as pltpu
from jax.sharding import PartitionSpec as P

NTR = 3
LEV = 10
HALO = 16
FEAT = 32
SENT = NTR * LEV
FAR_OUT = 1000.0
LANES = 128
FOUR = LANES // FEAT
EDGES = LANES // HALO
PEERS = 128
PIECE = 4
OUT_PIECES = 1
AXES = ("lon", "lat")
MESH = pl.DeviceIdType.MESH


def factor_levels(coefs):
    inverses, uppers = [], []
    for level in range(LEV):
        denom = jnp.ones_like(coefs[0])
        if level > 0:
            denom = denom + coefs[level - 1]
        if level < LEV - 1:
            denom = denom + coefs[level]
        if level > 0:
            denom = denom - coefs[level - 1] * uppers[level - 1]
        inverses.append(1.0 / denom)
        if level < LEV - 1:
            uppers.append(coefs[level] * inverses[level])
    return inverses, uppers


def solve_levels(values, coefs, inverses, uppers):
    reduced = []
    for level in range(LEV):
        right = values[level]
        if level > 0:
            right = right + coefs[level - 1] * reduced[level - 1]
        reduced.append(right * inverses[level])
    output = [None] * LEV
    output[LEV - 1] = reduced[LEV - 1]
    for level in range(LEV - 2, -1, -1):
        output[level] = reduced[level] + uppers[level] * output[level + 1]
    return output


def exchange_kernel(
    tracers_hbm, offsets_hbm, weights_hbm, diffusion_hbm, index_hbm, count_hbm, arrived, lengths,
    tracers, offsets, weights, diffusion, index, count, partial, factors,
    edge_low, edge_high, from_east, from_west, rows, table, stage, outbox, place, address,
    load_sems, edge_sems, address_sem, send_sem, recv_sem, ready, tracer_sems,
):
    pairs = (
        (index_hbm, index), (offsets_hbm, offsets),
        (weights_hbm, weights), (diffusion_hbm, diffusion), (count_hbm, count),
    )
    loads = [pltpu.make_async_copy(source, here, load_sems.at[i]) for i, (source, here) in enumerate(pairs)]
    def tracer_load(piece):
        at = pl.ds(piece * PIECE * 8, PIECE * 8)
        return pltpu.make_async_copy(tracers_hbm.at[:, :, at], tracers.at[:, :, at], tracer_sems.at[piece])

    for piece in range(tracers.shape[2] // (PIECE * 8)):
        tracer_load(piece).start()
    lat_rows = tracers.shape[2]
    groups = lat_rows // 8
    packs = from_east.shape[1]
    lon, lat = lax.axis_index("lon"), lax.axis_index("lat")
    bands = lax.axis_size("lon")
    me = lon * 2 + lat
    lane = lax.broadcasted_iota(jnp.int32, (8, LANES), 1)
    sublanes = lax.broadcasted_iota(jnp.int32, (8, LANES), 0)

    barrier = pltpu.get_barrier_semaphore()

    def digit_mates(low, span):
        mask = span - low
        return [(me & (PEERS - 1 - mask)) + ((me + low * step) & mask) for step in range(1, span // low)]

    def greet(semaphore, other):
        pl.semaphore_signal(semaphore, inc=1, device_id=(other >> 1, other & 1), device_id_type=MESH)

    ring = [(me + 2) & (PEERS - 1), (me - 2) & (PEERS - 1)]
    entrance = ring + digit_mates(1, 4) + digit_mates(4, 16) + digit_mates(16, PEERS)
    for other in entrance:
        greet(barrier, other)
    for load in loads:
        load.start()

    def pack_edges(group, carry):
        at = pl.ds(pl.multiple_of(group * 8, 8), 8)
        for pack in range(packs):
            low = high = None
            for part in range(EDGES):
                plane = pack * EDGES + part
                if plane >= NTR * LEV:
                    continue
                value = tracers[plane // LEV, plane % LEV, at, :]
                low_at = (part + EDGES // 2) % EDGES
                to_low = pltpu.roll(value, low_at * HALO, 1) if low_at else value
                to_high = pltpu.roll(value, (part + 1) * HALO, 1) if part + 1 < EDGES else value
                low = to_low if part == 0 else jnp.where(lane // HALO == low_at, to_low, low)
                high = to_high if part == 0 else jnp.where(lane // HALO == part, to_high, high)
            edge_low[group, pack] = low
            edge_high[group, pack] = high
        return carry

    def edge_copies(piece):
        part = pl.ds(piece * PIECE, PIECE)
        return [
            pltpu.make_async_remote_copy(
                src_ref=source.at[part], dst_ref=target.at[part],
                send_sem=edge_sems.at[side, 0, piece], recv_sem=edge_sems.at[side, 1, piece],
                device_id=(lax.rem(lon + distance, bands), lat), device_id_type=MESH,
            )
            for side, source, target, distance in ((0, edge_low, from_east, bands - 1), (1, edge_high, from_west, 1))
        ]

    pieces = groups // PIECE
    for piece in range(pieces):
        tracer_load(piece).wait()
        lax.fori_loop(piece * PIECE, piece * PIECE + PIECE, pack_edges, 0, unroll=True)
        if piece == 0:
            pl.semaphore_wait(barrier, len(entrance))
        for copy in edge_copies(piece):
            copy.start()
    for other in digit_mates(1, 4):
        greet(ready.at[0], other)

    loads[0].wait()
    column = index[...]
    owner = lax.broadcasted_iota(jnp.int32, column.shape, 0)
    member_of = (owner // 16 - lon // 8) & 3
    row = column >> 7
    turn_by = (member_of - row) & 3
    place[...] = turn_by * (lat_rows * LANES // 4) + (row >> 2) * LANES + (column & (LANES - 1))
    to_scalars = pltpu.make_async_copy(place, address, address_sem)
    to_scalars.start()

    for load in loads[1:]:
        load.wait()

    def interior(group, carry):
        at = pl.ds(pl.multiple_of(group * 8, 8), 8)
        for level in range(LEV):
            cell = lane + offsets[level, at, :]
            weight = weights[level, at, :]
            west_weight = jnp.where((cell >= 0) & (cell < LANES), 1.0 - weight, 0.0)
            east_weight = jnp.where((cell >= -1) & (cell < LANES - 1), weight, 0.0)
            west_at = cell & (LANES - 1)
            east_at = (cell + 1) & (LANES - 1)
            for t in range(NTR):
                main = tracers[t, level, at, :]
                west = jnp.take_along_axis(main, west_at, axis=1)
                east = jnp.take_along_axis(main, east_at, axis=1)
                partial[t, level, at, :] = west_weight * west + east_weight * east
        inverses, uppers = factor_levels([diffusion[level, at, :] for level in range(LEV - 1)])
        for level in range(LEV):
            factors[level, at, :] = inverses[level]
        for level in range(LEV - 1):
            factors[LEV + level, at, :] = uppers[level]
        return carry

    lax.fori_loop(0, groups, interior, 0, unroll=8)
    pl.semaphore_wait(ready.at[0], 3)
    for other in digit_mates(4, 16):
        greet(ready.at[1], other)

    def finish(group):
        at = pl.ds(group * 8, 8)
        values = [[None] * LEV for _ in range(NTR)]
        for level in range(LEV):
            cell = lane + offsets[level, at, :]
            weight = weights[level, at, :]
            west_weight = jnp.where((cell >= 0) & (cell < LANES), 0.0, 1.0 - weight)
            east_weight = jnp.where((cell >= -1) & (cell < LANES - 1), 0.0, weight)
            west_at = (cell & (HALO - 1)) + jnp.where(cell < 0, 0, LANES // 2)
            east_at = ((cell + 1) & (HALO - 1)) + jnp.where(cell < -1, 0, LANES // 2)
            for t in range(NTR):
                plane = t * LEV + level
                pack, part = plane // EDGES, plane % EDGES
                edge = jnp.where(lane // HALO == part, from_west[group, pack], from_east[group, pack])
                west = jnp.take_along_axis(edge, (west_at + part * HALO) & (LANES - 1), axis=1)
                east = jnp.take_along_axis(edge, (east_at + part * HALO) & (LANES - 1), axis=1)
                values[t][level] = partial[t, level, at, :] + (west_weight * west + east_weight * east)
        coefs = [diffusion[level, at, :] for level in range(LEV - 1)]
        inverses = [factors[level, at, :] for level in range(LEV)]
        uppers = [factors[LEV + level, at, :] for level in range(LEV - 1)]
        for t in range(NTR):
            solved = solve_levels(values[t], coefs, inverses, uppers)
            for level in range(LEV):
                rows[pl.ds(group * 8 * FEAT + level * NTR + t, 8, stride=FEAT), :] = solved[level]
        for spare in range(NTR * LEV, FEAT):
            rows[pl.ds(group * 8 * FEAT + spare, 8, stride=FEAT), :] = jnp.zeros((8, LANES), jnp.float32)

    def turn(block):
        at = pl.ds(block * LANES, LANES)
        turned = rows[at, :].T
        for by in range(FOUR):
            table[by, at, :] = pltpu.roll(turned, by * FEAT, 1) if by else turned

    blocks = PIECE * 8 // FOUR
    for piece in range(pieces + 1):
        if piece < pieces:
            for copy in edge_copies(piece):
                copy.wait_recv()
        for part in range(PIECE):
            if piece < pieces:
                finish(piece * PIECE + part)
            if piece:
                for block in range(blocks // PIECE):
                    turn((piece - 1) * blocks + part * (blocks // PIECE) + block)

    table_rows = table.reshape(FOUR * lat_rows * LANES // FOUR, LANES)

    x, y, z, core = (lon >> 3) & 3, lat * 2 + (lon >> 5), (lon >> 1) & 3, lon & 1

    def targets_of(step):
        away = step & 15
        to_core = (core + (step >> 4)) & 1
        targets = []
        for member in range(FOUR):
            to_x = (x + member) & 3
            to_y = (y + (away & 3) + member) & 3
            to_z = (z + ((away >> 2) + away) + member) & 3
            to_lon = ((to_y & 1) << 5) + (to_x << 3) + (to_z << 1) + to_core
            to_lat = to_y >> 1
            targets.append((to_lon, to_lat, to_lon * 2 + to_lat))
        return targets

    def gather(step, half):
        owners = [owner for _, _, owner in targets_of(step)]
        for eight in range(LANES // 8):
            wide = None
            for member in range(FOUR):
                tile = None
                for sublane in range(8):
                    at = address[owners[member], eight * 8 + sublane]
                    row = jnp.broadcast_to(table_rows[pl.ds(at, 1), :], (8, LANES))
                    tile = row if tile is None else jnp.where(sublanes == sublane, row, tile)
                wide = tile if wide is None else jnp.where(lane // FEAT == member, tile, wide)
            stage[half, eight * 8 : eight * 8 + 8, :] = wide

    def send(step, half):
        turned = stage[half].T
        for member, (to_lon, to_lat, owner) in enumerate(targets_of(step)):
            box = step * FOUR + member
            outbox[box] = turned[member * FEAT : (member + 1) * FEAT, :]
            length = jnp.full((1, LANES), count[0, owner].astype(jnp.float32), jnp.float32)
            unused = (lane[0:1] == LANES - 1) & (length < LANES)
            outbox[box, 0:1, :] = jnp.where(unused, length + FAR_OUT, turned[member * FEAT : member * FEAT + 1, :])
            slot = (owner - me) & (PEERS - 1)

            def start():
                pltpu.make_async_remote_copy(
                    src_ref=outbox.at[box, 0:SENT], dst_ref=arrived.at[slot, 0:SENT],
                    send_sem=send_sem, recv_sem=recv_sem,
                    device_id=(to_lon, to_lat), device_id_type=MESH,
                ).start()

            if member or half:
                start()
            else:
                pl.when(step > 0)(start)

    to_scalars.wait()
    pl.semaphore_wait(ready.at[1], 3)
    steps = PEERS // FOUR
    def two_steps(turn_at, carry):
        for half in range(2):
            gather(2 * turn_at + half, half)
            send(2 * turn_at + half, half)
        return carry

    lax.fori_loop(0, steps // 2, two_steps, 0)
    arrived[0] = outbox[0]
    others = pltpu.make_async_copy(outbox.at[1:PEERS, 0:SENT], arrived.at[1:PEERS, 0:SENT], recv_sem)
    others.wait()
    pltpu.make_async_copy(outbox.at[1:PEERS, 0:SENT], arrived.at[1:PEERS, 0:SENT], send_sem).wait()
    last = arrived[:, 0, :].T[LANES - 1 : LANES, :]
    lengths[...] = jnp.where(last > FAR_OUT / 2, last - FAR_OUT, LANES).astype(jnp.int32)
    for piece in range(pieces):
        for copy in edge_copies(piece):
            copy.wait_send()


def place_kernel(arrived, lengths, out, owned, rows, out_sems):
    columns = out.shape[2]
    lane = lax.broadcasted_iota(jnp.int32, (FEAT, LANES), 1)

    def place(source, start):
        block = start // LANES
        shift = lax.rem(start, LANES)
        rolled = pltpu.roll(arrived[source], shift, 1)
        first = pl.ds(pl.multiple_of(block * FEAT, FEAT), FEAT)
        second = pl.ds(pl.multiple_of(block * FEAT + FEAT, FEAT), FEAT)
        pltpu.store(owned.at[first, :], rolled, mask=lane >= shift)
        owned[second, :] = rolled
        return start + lengths[0, source]

    lax.fori_loop(0, arrived.shape[0], place, jnp.int32(0), unroll=128)

    copies = []
    width = columns // OUT_PIECES
    for piece in range(OUT_PIECES):
        for block in range(piece * width // LANES, (piece + 1) * width // LANES):
            for level in range(LEV):
                begin = block * FEAT + level * NTR
                rows[level, :, block * LANES : (block + 1) * LANES] = owned[begin : begin + NTR, :]
        part = pl.ds(piece * width, width)
        copies.append(pltpu.make_async_copy(rows.at[:, :, part], out.at[:, :, part], out_sems.at[piece]))
        copies[-1].start()
    for copy in copies:
        copy.wait()


def body(tracers, offsets, weights, diffusion, send_index, send_count):
    lat_rows, lon_width = tracers.shape[2:]
    columns = lat_rows * lon_width
    groups = lat_rows // 8
    packs = -(-NTR * LEV // EDGES)
    vmem = pl.BlockSpec(memory_space=pltpu.VMEM)
    smem = pl.BlockSpec(memory_space=pltpu.SMEM)
    edge = pltpu.VMEM((groups, packs, 8, LANES), jnp.float32)
    arrived, lengths = pl.pallas_call(
        exchange_kernel,
        out_shape=(
            jax.ShapeDtypeStruct((PEERS, FEAT, LANES), jnp.float32),
            jax.ShapeDtypeStruct((1, PEERS), jnp.int32),
        ),
        in_specs=[pl.BlockSpec(memory_space=pltpu.HBM)] * 6,
        out_specs=(vmem, vmem),
        scratch_shapes=[
            pltpu.VMEM(tracers.shape, jnp.float32),
            pltpu.VMEM(offsets.shape, jnp.int32),
            pltpu.VMEM(weights.shape, jnp.float32),
            pltpu.VMEM(diffusion.shape, jnp.float32),
            pltpu.VMEM((PEERS, LANES), jnp.int32),
            pltpu.SMEM((1, PEERS), jnp.int32),
            pltpu.VMEM(tracers.shape, jnp.float32),
            pltpu.VMEM((2 * LEV - 1, lat_rows, lon_width), jnp.float32),
            edge, edge, edge, edge,
            pltpu.VMEM((lat_rows * FEAT, LANES), jnp.float32),
            pltpu.VMEM((FOUR, columns // FOUR, LANES), jnp.float32),
            pltpu.VMEM((2, LANES, LANES), jnp.float32),
            pltpu.VMEM((PEERS, FEAT, LANES), jnp.float32),
            pltpu.VMEM((PEERS, LANES), jnp.int32),
            pltpu.SMEM((PEERS, LANES), jnp.int32),
            pltpu.SemaphoreType.DMA((5,)),
            pltpu.SemaphoreType.DMA((2, 2, groups // PIECE)),
            pltpu.SemaphoreType.DMA,
            pltpu.SemaphoreType.DMA,
            pltpu.SemaphoreType.DMA,
            pltpu.SemaphoreType.REGULAR((2,)),
            pltpu.SemaphoreType.DMA((groups // PIECE,)),
        ],
        compiler_params=pltpu.CompilerParams(vmem_limit_bytes=40 << 20, collective_id=0, has_side_effects=True),
        name="advect_solve_exchange",
    )(*(pltpu.with_memory_space_constraint(x, pltpu.HBM) for x in (tracers, offsets, weights, diffusion, send_index[0], send_count)))
    owned = pl.pallas_call(
        place_kernel,
        out_shape=jax.ShapeDtypeStruct((LEV, NTR, columns), jnp.float32),
        in_specs=[vmem, smem],
        out_specs=pl.BlockSpec(memory_space=pltpu.HBM),
        scratch_shapes=[
            pltpu.VMEM(((columns // LANES + 2) * FEAT, LANES), jnp.float32),
            pltpu.VMEM((LEV, NTR, columns), jnp.float32),
            pltpu.SemaphoreType.DMA((OUT_PIECES,)),
        ],
        compiler_params=pltpu.CompilerParams(vmem_limit_bytes=32 << 20),
        name="place_owned",
    )(arrived, lengths)
    return jnp.transpose(owned, (1, 0, 2))


def solution(mesh):
    return jax.shard_map(
        body,
        mesh=mesh,
        in_specs=(
            P(None, None, "lat", "lon"),
            P(None, "lat", "lon"),
            P(None, "lat", "lon"),
            P(None, "lat", "lon"),
            P(("lon", "lat"), None, None),
            P(("lon", "lat"), None),
        ),
        out_specs=P(None, None, ("lon", "lat")),
        check_vma=False,
    )
```

```python
import jax
import jax.numpy as jnp
from jax import lax
from jax.experimental import pallas as pl
from jax.experimental.pallas import tpu as pltpu
from jax.sharding import PartitionSpec as P

NTR = 3
LEV = 10
HALO = 16
FEAT = 32
SENT = NTR * LEV
FAR_OUT = 1000.0
LANES = 128
FOUR = LANES // FEAT
EDGES = LANES // HALO
PEERS = 128
PIECE = 4
OUT_PIECES = 1
AXES = ("lon", "lat")
MESH = pl.DeviceIdType.MESH


def factor_levels(coefs):
    inverses, uppers = [], []
    for level in range(LEV):
        denom = jnp.ones_like(coefs[0])
        if level > 0:
            denom = denom + coefs[level - 1]
        if level < LEV - 1:
            denom = denom + coefs[level]
        if level > 0:
            denom = denom - coefs[level - 1] * uppers[level - 1]
        inverses.append(1.0 / denom)
        if level < LEV - 1:
            uppers.append(coefs[level] * inverses[level])
    return inverses, uppers


def solve_levels(values, coefs, inverses, uppers):
    reduced = []
    for level in range(LEV):
        right = values[level]
        if level > 0:
            right = right + coefs[level - 1] * reduced[level - 1]
        reduced.append(right * inverses[level])
    output = [None] * LEV
    output[LEV - 1] = reduced[LEV - 1]
    for level in range(LEV - 2, -1, -1):
        output[level] = reduced[level] + uppers[level] * output[level + 1]
    return output


def exchange_kernel(
    tracers_hbm, offsets_hbm, weights_hbm, diffusion_hbm, index_hbm, count_hbm, arrived, lengths,
    tracers, offsets, weights, diffusion, index, count, partial, factors,
    edge_low, edge_high, from_east, from_west, rows, table, stage, outbox, place, address,
    load_sems, edge_sems, address_sem, send_sem, recv_sem, ready, tracer_sems,
):
    pairs = (
        (index_hbm, index), (offsets_hbm, offsets),
        (weights_hbm, weights), (diffusion_hbm, diffusion), (count_hbm, count),
    )
    loads = [pltpu.make_async_copy(source, here, load_sems.at[i]) for i, (source, here) in enumerate(pairs)]
    def tracer_load(piece):
        at = pl.ds(piece * PIECE * 8, PIECE * 8)
        return pltpu.make_async_copy(tracers_hbm.at[:, :, at], tracers.at[:, :, at], tracer_sems.at[piece])

    for piece in range(tracers.shape[2] // (PIECE * 8)):
        tracer_load(piece).start()
    lat_rows = tracers.shape[2]
    groups = lat_rows // 8
    packs = from_east.shape[1]
    lon, lat = lax.axis_index("lon"), lax.axis_index("lat")
    bands = lax.axis_size("lon")
    me = lon * 2 + lat
    lane = lax.broadcasted_iota(jnp.int32, (8, LANES), 1)
    sublanes = lax.broadcasted_iota(jnp.int32, (8, LANES), 0)

    barrier = pltpu.get_barrier_semaphore()

    def digit_mates(low, span):
        mask = span - low
        return [(me & (PEERS - 1 - mask)) + ((me + low * step) & mask) for step in range(1, span // low)]

    def greet(semaphore, other):
        pl.semaphore_signal(semaphore, inc=1, device_id=(other >> 1, other & 1), device_id_type=MESH)

    ring = [(me + 2) & (PEERS - 1), (me - 2) & (PEERS - 1)]
    entrance = ring + digit_mates(1, 4) + digit_mates(4, 16) + digit_mates(16, PEERS)
    for other in entrance:
        greet(barrier, other)
    for load in loads:
        load.start()

    def pack_edges(group, carry):
        at = pl.ds(pl.multiple_of(group * 8, 8), 8)
        for pack in range(packs):
            low = high = None
            for part in range(EDGES):
                plane = pack * EDGES + part
                if plane >= NTR * LEV:
                    continue
                value = tracers[plane // LEV, plane % LEV, at, :]
                low_at = (part + EDGES // 2) % EDGES
                to_low = pltpu.roll(value, low_at * HALO, 1) if low_at else value
                to_high = pltpu.roll(value, (part + 1) * HALO, 1) if part + 1 < EDGES else value
                low = to_low if part == 0 else jnp.where(lane // HALO == low_at, to_low, low)
                high = to_high if part == 0 else jnp.where(lane // HALO == part, to_high, high)
            edge_low[group, pack] = low
            edge_high[group, pack] = high
        return carry

    def edge_copies(piece):
        part = pl.ds(piece * PIECE, PIECE)
        return [
            pltpu.make_async_remote_copy(
                src_ref=source.at[part], dst_ref=target.at[part],
                send_sem=edge_sems.at[side, 0, piece], recv_sem=edge_sems.at[side, 1, piece],
                device_id=(lax.rem(lon + distance, bands), lat), device_id_type=MESH,
            )
            for side, source, target, distance in ((0, edge_low, from_east, bands - 1), (1, edge_high, from_west, 1))
        ]

    pieces = groups // PIECE
    for piece in range(pieces):
        tracer_load(piece).wait()
        lax.fori_loop(piece * PIECE, piece * PIECE + PIECE, pack_edges, 0, unroll=True)
        if piece == 0:
            pl.semaphore_wait(barrier, len(entrance))
        for copy in edge_copies(piece):
            copy.start()
    for other in digit_mates(1, 4):
        greet(ready.at[0], other)

    loads[0].wait()
    column = index[...]
    owner = lax.broadcasted_iota(jnp.int32, column.shape, 0)
    member_of = (owner // 16 - lon // 8) & 3
    row = column >> 7
    turn_by = (member_of - row) & 3
    place[...] = turn_by * (lat_rows * LANES // 4) + (row >> 2) * LANES + (column & (LANES - 1))
    to_scalars = pltpu.make_async_copy(place, address, address_sem)
    to_scalars.start()

    for load in loads[1:]:
        load.wait()

    def interior(group, carry):
        at = pl.ds(pl.multiple_of(group * 8, 8), 8)
        for level in range(LEV):
            cell = lane + offsets[level, at, :]
            weight = weights[level, at, :]
            west_weight = jnp.where((cell >= 0) & (cell < LANES), 1.0 - weight, 0.0)
            east_weight = jnp.where((cell >= -1) & (cell < LANES - 1), weight, 0.0)
            west_at = cell & (LANES - 1)
            east_at = (cell + 1) & (LANES - 1)
            for t in range(NTR):
                main = tracers[t, level, at, :]
                west = jnp.take_along_axis(main, west_at, axis=1)
                east = jnp.take_along_axis(main, east_at, axis=1)
                partial[t, level, at, :] = west_weight * west + east_weight * east
        inverses, uppers = factor_levels([diffusion[level, at, :] for level in range(LEV - 1)])
        for level in range(LEV):
            factors[level, at, :] = inverses[level]
        for level in range(LEV - 1):
            factors[LEV + level, at, :] = uppers[level]
        return carry

    lax.fori_loop(0, groups, interior, 0, unroll=8)
    pl.semaphore_wait(ready.at[0], 3)
    for other in digit_mates(4, 16):
        greet(ready.at[1], other)

    def finish(group):
        at = pl.ds(group * 8, 8)
        values = [[None] * LEV for _ in range(NTR)]
        for level in range(LEV):
            cell = lane + offsets[level, at, :]
            weight = weights[level, at, :]
            west_weight = jnp.where((cell >= 0) & (cell < LANES), 0.0, 1.0 - weight)
            east_weight = jnp.where((cell >= -1) & (cell < LANES - 1), 0.0, weight)
            west_at = (cell & (HALO - 1)) + jnp.where(cell < 0, 0, LANES // 2)
            east_at = ((cell + 1) & (HALO - 1)) + jnp.where(cell < -1, 0, LANES // 2)
            for t in range(NTR):
                plane = t * LEV + level
                pack, part = plane // EDGES, plane % EDGES
                edge = jnp.where(lane // HALO == part, from_west[group, pack], from_east[group, pack])
                west = jnp.take_along_axis(edge, (west_at + part * HALO) & (LANES - 1), axis=1)
                east = jnp.take_along_axis(edge, (east_at + part * HALO) & (LANES - 1), axis=1)
                values[t][level] = partial[t, level, at, :] + (west_weight * west + east_weight * east)
        coefs = [diffusion[level, at, :] for level in range(LEV - 1)]
        inverses = [factors[level, at, :] for level in range(LEV)]
        uppers = [factors[LEV + level, at, :] for level in range(LEV - 1)]
        for t in range(NTR):
            solved = solve_levels(values[t], coefs, inverses, uppers)
            for level in range(LEV):
                rows[pl.ds(group * 8 * FEAT + level * NTR + t, 8, stride=FEAT), :] = solved[level]
        for spare in range(NTR * LEV, FEAT):
            rows[pl.ds(group * 8 * FEAT + spare, 8, stride=FEAT), :] = jnp.zeros((8, LANES), jnp.float32)

    def turn(block):
        at = pl.ds(block * LANES, LANES)
        turned = rows[at, :].T
        for by in range(FOUR):
            table[by, at, :] = pltpu.roll(turned, by * FEAT, 1) if by else turned

    blocks = PIECE * 8 // FOUR
    for piece in range(pieces + 1):
        if piece < pieces:
            for copy in edge_copies(piece):
                copy.wait_recv()
        for part in range(PIECE):
            if piece < pieces:
                finish(piece * PIECE + part)
            if piece:
                for block in range(blocks // PIECE):
                    turn((piece - 1) * blocks + part * (blocks // PIECE) + block)

    table_rows = table.reshape(FOUR * lat_rows * LANES // FOUR, LANES)

    x, y, z, core = (lon >> 3) & 3, lat * 2 + (lon >> 5), (lon >> 1) & 3, lon & 1

    def targets_of(step):
        away = step & 15
        to_core = (core + (step >> 4)) & 1
        targets = []
        for member in range(FOUR):
            to_x = (x + member) & 3
            to_y = (y + (away & 3) + member) & 3
            to_z = (z + ((away >> 2) + away) + member) & 3
            to_lon = ((to_y & 1) << 5) + (to_x << 3) + (to_z << 1) + to_core
            to_lat = to_y >> 1
            targets.append((to_lon, to_lat, to_lon * 2 + to_lat))
        return targets

    def gather(step, half):
        owners = [owner for _, _, owner in targets_of(step)]
        for eight in range(LANES // 8):
            wide = None
            for member in range(FOUR):
                tile = None
                for sublane in range(8):
                    at = address[owners[member], eight * 8 + sublane]
                    row = table_rows[pl.ds(at, 8, stride=0), :]
                    tile = row if tile is None else jnp.where(sublanes == sublane, row, tile)
                wide = tile if wide is None else jnp.where(lane // FEAT == member, tile, wide)
            stage[half, eight * 8 : eight * 8 + 8, :] = wide

    def send(step, half):
        turned = stage[half].T
        for member, (to_lon, to_lat, owner) in enumerate(targets_of(step)):
            box = step * FOUR + member
            outbox[box] = turned[member * FEAT : (member + 1) * FEAT, :]
            length = jnp.full((1, LANES), count[0, owner].astype(jnp.float32), jnp.float32)
            unused = (lane[0:1] == LANES - 1) & (length < LANES)
            outbox[box, 0:1, :] = jnp.where(unused, length + FAR_OUT, turned[member * FEAT : member * FEAT + 1, :])
            slot = (owner - me) & (PEERS - 1)

            def start():
                pltpu.make_async_remote_copy(
                    src_ref=outbox.at[box, 0:SENT], dst_ref=arrived.at[slot, 0:SENT],
                    send_sem=send_sem, recv_sem=recv_sem,
                    device_id=(to_lon, to_lat), device_id_type=MESH,
                ).start()

            if member or half:
                start()
            else:
                pl.when(step > 0)(start)

    to_scalars.wait()
    pl.semaphore_wait(ready.at[1], 3)
    steps = PEERS // FOUR
    def two_steps(turn_at, carry):
        for half in range(2):
            gather(2 * turn_at + half, half)
            send(2 * turn_at + half, half)
        return carry

    lax.fori_loop(0, steps // 2, two_steps, 0)
    arrived[0] = outbox[0]
    others = pltpu.make_async_copy(outbox.at[1:PEERS, 0:SENT], arrived.at[1:PEERS, 0:SENT], recv_sem)
    others.wait()
    pltpu.make_async_copy(outbox.at[1:PEERS, 0:SENT], arrived.at[1:PEERS, 0:SENT], send_sem).wait()
    last = arrived[:, 0, :].T[LANES - 1 : LANES, :]
    lengths[...] = jnp.where(last > FAR_OUT / 2, last - FAR_OUT, LANES).astype(jnp.int32)
    for piece in range(pieces):
        for copy in edge_copies(piece):
            copy.wait_send()


def place_kernel(arrived, lengths, out, owned, rows, out_sems):
    columns = out.shape[2]
    lane = lax.broadcasted_iota(jnp.int32, (FEAT, LANES), 1)

    def place(source, start):
        block = start >> 7
        shift = start & (LANES - 1)
        rolled = pltpu.roll(arrived[source], shift, 1)
        first = pl.ds(pl.multiple_of(block * FEAT, FEAT), FEAT)
        second = pl.ds(pl.multiple_of(block * FEAT + FEAT, FEAT), FEAT)
        pltpu.store(owned.at[first, :], rolled, mask=lane >= shift)
        owned[second, :] = rolled
        return start + lengths[0, source]

    lax.fori_loop(0, arrived.shape[0], place, jnp.int32(0), unroll=128)

    copies = []
    width = columns // OUT_PIECES
    for piece in range(OUT_PIECES):
        for block in range(piece * width // LANES, (piece + 1) * width // LANES):
            for level in range(LEV):
                begin = block * FEAT + level * NTR
                rows[level, :, block * LANES : (block + 1) * LANES] = owned[begin : begin + NTR, :]
        part = pl.ds(piece * width, width)
        copies.append(pltpu.make_async_copy(rows.at[:, :, part], out.at[:, :, part], out_sems.at[piece]))
        copies[-1].start()
    for copy in copies:
        copy.wait()


def body(tracers, offsets, weights, diffusion, send_index, send_count):
    lat_rows, lon_width = tracers.shape[2:]
    columns = lat_rows * lon_width
    groups = lat_rows // 8
    packs = -(-NTR * LEV // EDGES)
    vmem = pl.BlockSpec(memory_space=pltpu.VMEM)
    smem = pl.BlockSpec(memory_space=pltpu.SMEM)
    edge = pltpu.VMEM((groups, packs, 8, LANES), jnp.float32)
    arrived, lengths = pl.pallas_call(
        exchange_kernel,
        out_shape=(
            jax.ShapeDtypeStruct((PEERS, FEAT, LANES), jnp.float32),
            jax.ShapeDtypeStruct((1, PEERS), jnp.int32),
        ),
        in_specs=[pl.BlockSpec(memory_space=pltpu.HBM)] * 6,
        out_specs=(vmem, vmem),
        scratch_shapes=[
            pltpu.VMEM(tracers.shape, jnp.float32),
            pltpu.VMEM(offsets.shape, jnp.int32),
            pltpu.VMEM(weights.shape, jnp.float32),
            pltpu.VMEM(diffusion.shape, jnp.float32),
            pltpu.VMEM((PEERS, LANES), jnp.int32),
            pltpu.SMEM((1, PEERS), jnp.int32),
            pltpu.VMEM(tracers.shape, jnp.float32),
            pltpu.VMEM((2 * LEV - 1, lat_rows, lon_width), jnp.float32),
            edge, edge, edge, edge,
            pltpu.VMEM((lat_rows * FEAT, LANES), jnp.float32),
            pltpu.VMEM((FOUR, columns // FOUR, LANES), jnp.float32),
            pltpu.VMEM((2, LANES, LANES), jnp.float32),
            pltpu.VMEM((PEERS, FEAT, LANES), jnp.float32),
            pltpu.VMEM((PEERS, LANES), jnp.int32),
            pltpu.SMEM((PEERS, LANES), jnp.int32),
            pltpu.SemaphoreType.DMA((5,)),
            pltpu.SemaphoreType.DMA((2, 2, groups // PIECE)),
            pltpu.SemaphoreType.DMA,
            pltpu.SemaphoreType.DMA,
            pltpu.SemaphoreType.DMA,
            pltpu.SemaphoreType.REGULAR((2,)),
            pltpu.SemaphoreType.DMA((groups // PIECE,)),
        ],
        compiler_params=pltpu.CompilerParams(vmem_limit_bytes=40 << 20, collective_id=0, has_side_effects=True),
        name="advect_solve_exchange",
    )(*(pltpu.with_memory_space_constraint(x, pltpu.HBM) for x in (tracers, offsets, weights, diffusion, send_index[0], send_count)))
    owned = pl.pallas_call(
        place_kernel,
        out_shape=jax.ShapeDtypeStruct((LEV, NTR, columns), jnp.float32),
        in_specs=[vmem, smem],
        out_specs=pl.BlockSpec(memory_space=pltpu.HBM),
        scratch_shapes=[
            pltpu.VMEM(((columns // LANES + 2) * FEAT, LANES), jnp.float32),
            pltpu.VMEM((LEV, NTR, columns), jnp.float32),
            pltpu.SemaphoreType.DMA((OUT_PIECES,)),
        ],
        compiler_params=pltpu.CompilerParams(vmem_limit_bytes=32 << 20),
        name="place_owned",
    )(arrived, lengths)
    return jnp.transpose(owned, (1, 0, 2))


def solution(mesh):
    return jax.shard_map(
        body,
        mesh=mesh,
        in_specs=(
            P(None, None, "lat", "lon"),
            P(None, "lat", "lon"),
            P(None, "lat", "lon"),
            P(None, "lat", "lon"),
            P(("lon", "lat"), None, None),
            P(("lon", "lat"), None),
        ),
        out_specs=P(None, None, ("lon", "lat")),
        check_vma=False,
    )
```
